128 devices in a mesh: dom: 8 (over y, core), narrow: 16 (over z, x).
Axes of the slice: x: 4, y: 4, z: 4, core: 2. Of those that a mesh axis runs over, the one named last changes fastest.
Arguments:
- feats: bfloat16 [131072, 768], P(('dom', 'narrow')), may hold values from -21 to 21
- node_type: int32 [1024], P('dom'), may hold values from 0 to 2
- tiles: int32 [1024, 4], P('dom'), may hold values from 0 to 127, as said below
- relation: int32 [1024, 4], P(('dom', 'narrow')), may hold values from 0 to 4
- neg_sched: int32 [128, 8], P('dom'), may hold values from 0 to 7
- w_query: bfloat16 [3, 768, 768], replicated, may hold values from -0.21875 to 0.21875
- w_key: bfloat16 [3, 768, 768], replicated, may hold values from -0.21875 to 0.21875
- w_value: bfloat16 [3, 768, 768], replicated, may hold values from -0.21875 to 0.21875
- w_out: bfloat16 [3, 768, 768], replicated, may hold values from -0.21875 to 0.21875
- rel_att: bfloat16 [5, 8, 96, 96], replicated, may hold values from -0.625 to 0.625
- rel_msg: bfloat16 [5, 8, 96, 96], replicated, may hold values from -0.625 to 0.625
- rel_prior: float32 [5, 8], replicated, may hold values from 0.5 to 2
- skip_gate: float32 [3], replicated, may hold values from -2 to 2
- pos_view: bfloat16 [131072, 768], P(('dom', 'narrow')), may hold values from -6 to 6
- type_weight: float32 [3], replicated, may hold values from 0.5 to 2
Outputs:
- embedding: bfloat16 [131072, 768], P(('dom', 'narrow'))
- node_loss: float32 [131072], P(('dom', 'narrow'))
- mean_loss: float32 [], replicated
The draws below stay inside these ranges and needn't reach their ends.
Inputs may be any that keep to these rules, and one draw needn't show every extreme that they name: `tiles`: values are block numbers within the target block's group: owner lane times 8 plus the owner's local block. Among the 32 entries of one device's target blocks, at most 3 name blocks of any one lane.
All inputs are finite; a program needn't handle non-finite values.
Results may differ from the reference program's by a relative error of at most 0.008.
The reference program's roundings to bfloat16 on the way (of `attention` and `activated`) count: a program that leaves them out, or rounds other values in their place, can miss the bound.
Values may be sent and summed in bfloat16 or wider, within the bound.
A program may use at most 128 MiB of HBM per device.

```python
import math
import jax
import jax.numpy as jnp
from jax import lax

D = 768
HEADS = 8
DH = 96
NTYPE = 3
NREL = 5
TILE = 128
NT = 4
TBLK = 8
NODES = 131072
CAP = 3
NEG_STEPS = 8
N_DOM = 8
N_NARROW = 16
DEVICES = 128


def draw_feats(key, part):
    base_key = jax.random.fold_in(jax.random.fold_in(key, 5), 0)
    return jax.random.truncated_normal(base_key, -6.0, 6.0, (NODES, D), jnp.float32).astype(jnp.bfloat16)


def request_owners(device_key):
    hot_key, star_key, base_key, perm_key, tile_key = jax.random.split(device_key, 5)
    slots_all = N_NARROW * CAP
    requests = TBLK * NT
    slot_owner = jnp.arange(slots_all, dtype=jnp.int32) // CAP
    hot_owner = jax.random.randint(hot_key, (2,), 0, N_NARROW)
    star_owner = jax.random.randint(star_key, (), 0, N_NARROW)
    is_hot = jnp.any(slot_owner[:, None] == hot_owner[None, :], axis=1).astype(jnp.int32)
    is_star = (slot_owner == star_owner).astype(jnp.int32)
    scores = jax.random.randint(base_key, (slots_all,), 0, 4096) + 2048 * is_hot + 65536 * is_star
    ranked = jnp.argsort(-(scores * slots_all + jnp.arange(slots_all, dtype=jnp.int32)))
    owners = slot_owner[ranked[:requests]]
    owners = owners[jax.random.permutation(perm_key, requests)]
    local_block = jax.random.randint(tile_key, (requests,), 0, TBLK)
    return (owners * TBLK + local_block).reshape(TBLK, NT)


def draw_tiles(key, part):
    device_keys = jax.random.split(jax.random.fold_in(key, 17), N_DOM * N_NARROW)
    per_device = jax.vmap(request_owners)(device_keys)
    return per_device.reshape(N_DOM * N_NARROW * TBLK, NT).astype(jnp.int32)


def with_ends(result, own_key, low, high):
    shape = result.shape
    index_at = [jax.random.randint(jax.random.fold_in(own_key, axis), (), 0, shape[axis]) for axis in range(len(shape))]
    result = result.at[tuple(index_at)].set(low)
    longest = shape.index(max(shape))
    index_at[longest] = (index_at[longest] + 1) % shape[longest]
    return result.at[tuple(index_at)].set(high)


def levels(own_key, dims, cuts, least, high):
    gain = 1.0
    for position, blocks in cuts:
        heights = jax.random.uniform(jax.random.fold_in(jax.random.fold_in(own_key, 6), position), (blocks,), jnp.float32, least / len(cuts), high / len(cuts))
        gain = gain * jnp.repeat(jnp.exp(heights), dims[position] // blocks).reshape((-1,) + (1,) * (len(dims) - 1 - position))
    return gain


def gaussian(stream_key, shape, deviation, limit, pieces=(), held_as=jnp.bfloat16):
    gain = levels(stream_key, shape, pieces, -0.22, 0.18) if pieces else 1.0
    drawn = jax.random.normal(stream_key, shape, jnp.float32) * deviation * gain
    return jnp.minimum(jnp.maximum(drawn, -limit), limit).astype(held_as)


def setup_inputs(seed: int = 0) -> dict:
    seeds = jax.random.split(jax.random.key(seed), 16)
    feats = draw_feats(jax.random.fold_in(seeds[15], 71), 0)
    node_type = with_ends(jax.random.randint(seeds[1], (NODES // TILE,), 0, NTYPE), jax.random.fold_in(seeds[1], 1), 0, NTYPE - 1).astype(jnp.int32)
    tiles = draw_tiles(jax.random.fold_in(seeds[15], 71), 0)
    relation = with_ends(jax.random.randint(seeds[3], (NODES // TILE, NT), 0, NREL), jax.random.fold_in(seeds[3], 1), 0, NREL - 1).astype(jnp.int32)
    neg_sched = with_ends(jax.random.randint(seeds[4], (DEVICES, NEG_STEPS), 0, TBLK), jax.random.fold_in(seeds[4], 1), 0, TBLK - 1).astype(jnp.int32)
    w_query = gaussian(seeds[5], (NTYPE, D, D), D ** -0.5, 0.21875)
    w_key = gaussian(seeds[6], (NTYPE, D, D), D ** -0.5, 0.21875)
    w_value = gaussian(seeds[7], (NTYPE, D, D), D ** -0.5, 0.21875)
    w_out = gaussian(seeds[8], (NTYPE, D, D), D ** -0.5, 0.21875)
    rel_att = gaussian(seeds[9], (NREL, HEADS, DH, DH), DH ** -0.5, 0.625)
    rel_msg = gaussian(seeds[10], (NREL, HEADS, DH, DH), DH ** -0.5, 0.625)
    rel_prior = jnp.clip(jnp.exp(jax.random.uniform(seeds[11], (NREL, HEADS), jnp.float32, math.log(0.5), math.log(2.0))), 0.5, 2.0)
    skip_gate = jnp.clip(jax.random.uniform(seeds[12], (NTYPE,), jnp.float32, -2.0, 2.0), -2.0, 2.0)
    pos_view = gaussian(seeds[13], (NODES, D), 1.0, 6.0, ((0, 128),))
    type_weight = jnp.clip(jnp.exp(jax.random.uniform(seeds[14], (NTYPE,), jnp.float32, math.log(0.5), math.log(2.0))), 0.5, 2.0)
    return {"feats": feats, "node_type": node_type, "tiles": tiles, "relation": relation, "neg_sched": neg_sched, "w_query": w_query, "w_key": w_key, "w_value": w_value, "w_out": w_out, "rel_att": rel_att, "rel_msg": rel_msg, "rel_prior": rel_prior, "skip_gate": skip_gate, "pos_view": pos_view, "type_weight": type_weight}


def rounded(values):
    return lax.optimization_barrier(values.astype(jnp.bfloat16))

def reference(feats, node_type, tiles, relation, neg_sched, w_query, w_key, w_value, w_out, rel_att, rel_msg, rel_prior, skip_gate, pos_view, type_weight):
    nblocks = NODES // TILE
    blocks = feats.reshape(nblocks, TILE, D)

    def project(inputs):
        block_rows, type_id = inputs
        return tuple((rounded(jnp.dot(block_rows, weight[type_id], preferred_element_type=jnp.float32)) for weight in (w_query, w_key, w_value)))
    queries, keys_all, values_all = lax.map(project, (blocks, node_type))
    group_size = N_NARROW * TBLK
    block_ids = jnp.arange(nblocks, dtype=jnp.int32)
    sources = tiles + (block_ids // group_size * group_size)[:, None]

    def attend(inputs):
        query_block, own_rows, source_ids, rel_ids, type_id = inputs
        src_keys = keys_all[source_ids].reshape(NT, TILE, HEADS, DH).astype(jnp.float32)
        src_values = values_all[source_ids].reshape(NT, TILE, HEADS, DH).astype(jnp.float32)
        keyed_rows = rounded(jnp.einsum('jmhd,jhde->jmhe', src_keys, rel_att[rel_ids].astype(jnp.float32), precision=lax.Precision.HIGHEST))
        message = rounded(jnp.einsum('jmhd,jhde->jmhe', src_values, rel_msg[rel_ids].astype(jnp.float32), precision=lax.Precision.HIGHEST))
        heads_query = query_block.reshape(TILE, HEADS, DH).astype(jnp.float32)
        scores = jnp.einsum('ihd,jmhd->hijm', heads_query, keyed_rows.astype(jnp.float32), precision=lax.Precision.HIGHEST)
        prior_scale = jnp.transpose(rel_prior[rel_ids]) / math.sqrt(DH)
        scores = (scores * prior_scale[:, None, :, None]).reshape(HEADS, TILE, NT * TILE)
        highest = lax.optimization_barrier(jnp.max(scores, axis=2, keepdims=True))
        exponent = jnp.exp(scores - highest)
        attention = rounded(exponent / lax.optimization_barrier(jnp.sum(exponent, axis=2, keepdims=True)))
        merged = jnp.einsum('hin,nhe->ihe', attention.astype(jnp.float32), message.reshape(NT * TILE, HEADS, DH).astype(jnp.float32), precision=lax.Precision.HIGHEST)
        activated = jax.nn.gelu(merged.reshape(TILE, D), approximate=False).astype(jnp.bfloat16)
        projected = jnp.dot(activated, w_out[type_id], preferred_element_type=jnp.float32)
        mix_gate = jax.nn.sigmoid(skip_gate[type_id])
        return (mix_gate * projected + (1.0 - mix_gate) * own_rows.astype(jnp.float32)).astype(jnp.bfloat16)
    out_blocks = lax.map(attend, (queries, blocks, sources, relation, node_type))
    device_of = block_ids // TBLK
    group_of = device_of // N_NARROW
    lane_of = device_of % N_NARROW
    offsets = jnp.arange(1, NEG_STEPS + 1, dtype=jnp.int32)
    sender = group_of[:, None] * N_NARROW + (lane_of[:, None] - offsets[None, :]) % N_NARROW
    neg_ids = (sender * TBLK + neg_sched[sender, offsets[None, :] - 1]).astype(jnp.int32)

    def contrast(inputs):
        own_out, own_pos, neg_block_ids, type_id = inputs
        own_float = own_out.astype(jnp.float32)
        positive = lax.optimization_barrier(jnp.sum(own_float * own_pos.astype(jnp.float32), axis=1)) / math.sqrt(D)
        neg_rows = out_blocks[neg_block_ids].reshape(NEG_STEPS * TILE, D).astype(jnp.float32)
        neg_logits = jnp.einsum('nd,md->nm', own_float, neg_rows, precision=lax.Precision.HIGHEST) / math.sqrt(D)
        same_type = jnp.repeat(node_type[neg_block_ids] == type_id, TILE, total_repeat_length=NEG_STEPS * TILE)
        neg_logits = jnp.where(same_type[None, :], neg_logits, -jnp.inf)
        highest = jnp.maximum(positive, lax.optimization_barrier(jnp.max(neg_logits, axis=1)))
        denominator = jnp.exp(positive - highest) + lax.optimization_barrier(jnp.sum(jnp.exp(neg_logits - highest[:, None]), axis=1))
        return highest + jnp.log(denominator) - positive
    node_loss = lax.map(contrast, (out_blocks, pos_view.reshape(nblocks, TILE, D), neg_ids, node_type)).reshape(NODES)
    row_weight = jnp.repeat(type_weight[node_type], TILE, total_repeat_length=NODES)
    mean_loss = jnp.sum(row_weight * node_loss) / NODES
    return (out_blocks.reshape(NODES, D), node_loss, mean_loss)
```

```python
import functools
import math

import jax
import jax.numpy as jnp
from jax import lax
from jax.experimental import pallas as pl
from jax.experimental.pallas import tpu as pltpu
from jax.sharding import Mesh
from jax.sharding import PartitionSpec as P

D = 768
HEADS = 8
DH = 96
TILE = 128
HALF = TILE // 2
NT = 4
NB = 8
REQ = NB * NT
RING = 4
CAP = 3
NREL = 5
STEPS = 8
LANES = 16
WIN = 256
WINDOW = [0, 0, 128, 256, 256, 384, 512, 512]
STRIP = [(0, 384), (128, 640), (384, 768)]
DOM_NARROW = ("dom_0", "dom_1", "narrow_0", "narrow_1")
DOM = ("dom_0", "dom_1")
MESH = pl.DeviceIdType.MESH
BF = jnp.bfloat16
F32 = jnp.float32

SEL = 0
IDX = 72
STYPE = 136
RELA = 168
OTYPE = 200
SCHED = 208
NTYP = 216
TABLE = 224


def prep_kernel(tiles, types, relation, sched, out, count):
    z = lax.axis_index("narrow_0")
    x = lax.axis_index("narrow_1")
    lane = z * RING + x

    def clear(i, c):
        out[SEL + i] = 0
        return c

    lax.fori_loop(0, 72, clear, 0)

    def scan(dst, visit):
        def zero(i, c):
            count[i] = 0
            return c

        lax.fori_loop(0, LANES, zero, 0)

        def body(p, c):
            t = tiles[dst * REQ + p]
            owner = t // NB
            k = count[owner]
            count[owner] = k + 1
            visit(p, t, owner, t % NB, k)
            return c

        lax.fori_loop(0, REQ, body, 0)

    def mine(p, t, owner, blk, k):
        oz = (z - owner // RING) % RING
        ox = (x - owner % RING) % RING
        out[IDX + p] = jnp.where(
            oz == 0, ox * NB + blk, 32 + (oz - 1) * 12 + ox * CAP + k
        )
        out[IDX + REQ + p] = jnp.where(
            ox == 0, oz * NB + blk, 32 + (ox - 1) * 12 + oz * CAP + k
        )
        out[STYPE + p] = types[t]
        out[RELA + p] = relation[p]

    scan(lane, mine)
    for d in range(1, RING):

        def row(p, t, owner, blk, k, d=d):
            @pl.when(owner // RING == z)
            def _():
                out[SEL + (d - 1) * 12 + (x - owner % RING) % RING * CAP + k] = blk

        scan((z + d) % RING * RING + x, row)

        def col(p, t, owner, blk, k, d=d):
            @pl.when(owner % RING == x)
            def _():
                out[SEL + 36 + (d - 1) * 12 + (z - owner // RING) % RING * CAP + k] = blk

        scan(z * RING + (x + d) % RING, col)
    for b in range(NB):
        out[OTYPE + b] = types[lane * NB + b]
    for s in range(STEPS):
        out[SCHED + s] = sched[lane * STEPS + s]
        frm = (lane - s - 1 + LANES) % LANES
        out[NTYP + s] = types[frm * NB + sched[frm * STEPS + s]]


def prep(tiles, types, relation, sched):
    smem = pl.BlockSpec(memory_space=pltpu.SMEM)
    return pl.pallas_call(
        prep_kernel,
        name="prep",
        out_shape=jax.ShapeDtypeStruct((TABLE,), jnp.int32),
        in_specs=[smem] * 4,
        out_specs=smem,
        scratch_shapes=[pltpu.SMEM((LANES,), jnp.int32)],
    )(tiles.reshape(-1), types, relation.reshape(-1), sched.reshape(-1))


def exchange_kernel(tab, feats, out, held, near, far, send, transit, lsem, s1, r1, s2, r2):
    coord = [lax.axis_index("narrow_1"), lax.axis_index("narrow_0")]
    name = ["narrow_1", "narrow_0"]

    def to(axis, by):
        return {name[axis]: (coord[axis] + by) % RING}

    local = [
        pltpu.make_async_copy(
            feats.at[:, pl.ds(rt * HALF, HALF), :], near.at[rt, pl.ds(0, NB)], lsem.at[rt]
        )
        for rt in range(2)
    ]
    for c in local:
        c.start()
    barrier = pltpu.get_barrier_semaphore()
    for axis in range(2):
        for by in (1, 3):
            pl.semaphore_signal(barrier, 1, device_id=to(axis, by), device_id_type=MESH)
    pl.semaphore_wait(barrier, 4)
    for c in local:
        c.wait()

    def first(rt, way, part):
        by = slot = (1, 3)[way]
        half = part if way == 0 else 1 - part
        return pltpu.make_async_remote_copy(
            src_ref=near.at[rt, pl.ds(half * 4, 4)],
            dst_ref=near.at[rt, pl.ds(slot * NB + half * 4, 4)],
            send_sem=s1.at[rt, way, part],
            recv_sem=r1.at[rt, way, part],
            device_id=to(rt, by),
            device_id_type=MESH,
        )

    def forward(rt, way):
        by = slot = (1, 3)[way]
        return pltpu.make_async_remote_copy(
            src_ref=near.at[rt, pl.ds(slot * NB + way * 4, 4)],
            dst_ref=near.at[rt, pl.ds(2 * NB + way * 4, 4)],
            send_sem=s1.at[rt, way, 2],
            recv_sem=r1.at[rt, way, 2],
            device_id=to(rt, by),
            device_id_type=MESH,
        )

    def second(rt, d, o):
        at = pl.ds((d - 1) * 12 + o * CAP, CAP)
        if d == 2:
            dst = transit.at[rt, pl.ds(o * CAP, CAP)]
            by = 1 if o < 2 else 3
        else:
            dst = far.at[rt, at]
            by = d
        return pltpu.make_async_remote_copy(
            src_ref=send.at[rt, at],
            dst_ref=dst,
            send_sem=s2.at[rt, d - 1, o],
            recv_sem=r2.at[rt, d - 1, o],
            device_id=to(1 - rt, by),
            device_id_type=MESH,
        )

    def onward(rt, o):
        return pltpu.make_async_remote_copy(
            src_ref=transit.at[rt, pl.ds(o * CAP, CAP)],
            dst_ref=far.at[rt, pl.ds(12 + o * CAP, CAP)],
            send_sem=s2.at[rt, 3, o],
            recv_sem=r2.at[rt, 3, o],
            device_id=to(1 - rt, 1 if o < 2 else 3),
            device_id_type=MESH,
        )

    def keep(rt, o):
        held[rt, o * NB : (o + 1) * NB] = near[rt, o * NB : (o + 1) * NB]

    def keep_far(rt, d, o):
        at = (d - 1) * 12 + o * CAP
        held[rt, 32 + at : 32 + at + CAP] = far[rt, at : at + CAP]

    def pick(rt, o):
        for d in (2, 1, 3):
            for k in range(CAP):
                at = (d - 1) * 12 + o * CAP + k
                blk = tab[SEL + rt * 36 + at]
                send[rt, at] = held[rt, o * NB + blk]
            second(rt, d, o).start()

    for part in range(2):
        for rt in range(2):
            for way in range(2):
                first(rt, way, part).start()
    for rt in range(2):
        keep(rt, 0)
        pick(rt, 0)
    for rt in range(2):
        for way in range(2):
            first(rt, way, 0).wait_recv()
            forward(rt, way).start()
    for rt in range(2):
        second(rt, 2, 0).wait_recv()
        onward(rt, 0).start()
    for o, way in ((1, 0), (3, 1)):
        for rt in range(2):
            first(rt, way, 1).wait_recv()
            keep(rt, o)
            pick(rt, o)
    for rt in range(2):
        for way in range(2):
            forward(rt, way).wait_recv()
        keep(rt, 2)
        pick(rt, 2)
    for o in (1, 3, 2):
        for rt in range(2):
            second(rt, 2, o).wait_recv()
            onward(rt, o).start()
    for o in (0, 1, 3, 2):
        for rt in range(2):
            for d in (1, 3):
                second(rt, d, o).wait_recv()
                keep_far(rt, d, o)
            onward(rt, o).wait_recv()
            keep_far(rt, 2, o)

    def collect(p, c):
        out[p, 0:HALF, :] = held[0, tab[IDX + p]]
        out[p, HALF:TILE, :] = held[1, tab[IDX + REQ + p]]
        return c

    lax.fori_loop(0, REQ, collect, 0)
    for rt in range(2):
        for way in range(2):
            for part in range(2):
                first(rt, way, part).wait_send()
            forward(rt, way).wait_send()
        for o in range(4):
            for d in (1, 2, 3):
                second(rt, d, o).wait_send()
            onward(rt, o).wait_send()


def exchange(table, feats):
    return pl.pallas_call(
        exchange_kernel,
        name="exchange",
        out_shape=jax.ShapeDtypeStruct((REQ, TILE, D), BF),
        in_specs=[
            pl.BlockSpec(memory_space=pltpu.SMEM),
            pl.BlockSpec(memory_space=pl.ANY),
        ],
        out_specs=pl.BlockSpec(memory_space=pltpu.VMEM),
        scratch_shapes=[
            pltpu.VMEM((2, 68, HALF, D), BF),
            pltpu.VMEM((2, 32, HALF, D), BF),
            pltpu.VMEM((2, 36, HALF, D), BF),
            pltpu.VMEM((2, 36, HALF, D), BF),
            pltpu.VMEM((2, 12, HALF, D), BF),
            pltpu.SemaphoreType.DMA((2,)),
            pltpu.SemaphoreType.DMA((2, 2, 3)),
            pltpu.SemaphoreType.DMA((2, 2, 3)),
            pltpu.SemaphoreType.DMA((2, 4, 4)),
            pltpu.SemaphoreType.DMA((2, 4, 4)),
        ],
        compiler_params=pltpu.CompilerParams(
            collective_id=0, has_side_effects=True, vmem_limit_bytes=60 << 20
        ),
    )(table, feats)


def dot(a, b):
    return jnp.dot(a, b, preferred_element_type=F32)


def dot_t(a, b):
    return lax.dot_general(a, b, (((1,), (1,)), ((), ())), preferred_element_type=F32)


STRIP_AT = [0, 384, 896]
STRIPS = 1280


def head_of(index):
    return sum((index >= DH * h).astype(jnp.int32) for h in range(1, HEADS))


def widen(rel, wide):
    for c, (lo, hi) in enumerate(STRIP):
        col = lax.broadcasted_iota(jnp.int32, (DH, WIN), 1) + c * WIN
        row = lax.broadcasted_iota(jnp.int32, (DH, WIN), 0)
        place = (col - DH * head_of(col) == row).astype(F32).astype(BF)
        full = dot(rel[lo:hi, :], place)
        col = lax.broadcasted_iota(jnp.int32, (hi - lo, WIN), 1) + c * WIN
        row = lax.broadcasted_iota(jnp.int32, (hi - lo, WIN), 0) + lo
        full = jnp.where(head_of(row) == head_of(col), full, 0.0)
        wide[STRIP_AT[c] : STRIP_AT[c] + hi - lo, :] = full.astype(BF)


def spread(rows, wide):
    return jnp.concatenate(
        [
            dot(rows[:, lo:hi], wide[STRIP_AT[c] : STRIP_AT[c] + hi - lo, :])
            for c, (lo, hi) in enumerate(STRIP)
        ],
        axis=1,
    ).astype(BF)


def attend_kernel(
    tab, prior, gate, blocks, fetched, wq, wk, wv, wo, att, msg, out,
    keyed, message, agg, att_wide, msg_wide
):
    b = pl.program_id(0)

    @pl.when(b == 0)
    def _():
        def body(r, c):
            widen(att.at[r], att_wide.at[r])
            widen(msg.at[r], msg_wide.at[r])
            return c

        lax.fori_loop(0, NREL, body, 0)

    tb = tab[OTYPE + b]
    rows = blocks[0]
    query = dot(rows, wq[tb]).astype(BF)
    for j in range(NT):
        ts = tab[STYPE + b * NT + j]
        r = tab[RELA + b * NT + j]
        src = fetched[j]
        key = dot(src, wk[ts]).astype(BF)
        value = dot(src, wv[ts]).astype(BF)
        at = pl.ds(j * TILE, TILE)
        keyed[at, :] = spread(key, att_wide.at[r])
        message[at, :] = spread(value, msg_wide.at[r])
    agg[...] = jnp.zeros_like(agg)
    column = lax.broadcasted_iota(jnp.int32, (TILE, WIN), 1)
    for h in range(HEADS):
        w = WINDOW[h]
        lo = h * DH - w
        mine = (column >= lo) & (column < lo + DH)
        q = jnp.where(mine, query[:, w : w + WIN].astype(F32), 0.0).astype(BF)
        scores = []
        for j in range(NT):
            scale = prior[tab[RELA + b * NT + j] * HEADS + h] * (1.0 / math.sqrt(DH))
            s = dot_t(q, keyed[j * TILE : (j + 1) * TILE, w : w + WIN])
            scores.append(s * scale)
        top = jnp.maximum(jnp.maximum(scores[0], scores[1]), jnp.maximum(scores[2], scores[3]))
        top = jnp.max(top, axis=1, keepdims=True)
        weights = [jnp.exp(s - top) for s in scores]
        total = jnp.sum((weights[0] + weights[1]) + (weights[2] + weights[3]), axis=1, keepdims=True)
        inv = 1.0 / total
        attention = jnp.concatenate([(e * inv).astype(BF) for e in weights], axis=1)
        got = dot(attention, message[:, w : w + WIN])
        agg[:, w : w + WIN] += jnp.where(mine, got, 0.0)
    merged = agg[...]
    active = (0.5 * merged * (1.0 + lax.erf(merged * math.sqrt(0.5)))).astype(BF)
    projected = dot(active, wo[tb])
    a = jax.nn.sigmoid(jnp.full((1, D), gate[tb], F32))
    out[0] = (a * projected + (1.0 - a) * rows.astype(F32)).astype(BF)


def attend(table, prior, gate, blocks, fetched, wq, wk, wv, wo, att, msg):
    def whole(shape):
        return pl.BlockSpec(
            shape, lambda b, *_: (0,) * len(shape), pipeline_mode=pl.Buffered(1)
        )

    weight = whole((3, D, D))
    wide = whole((NREL, D, DH))
    return pl.pallas_call(
        attend_kernel,
        name="attend",
        out_shape=jax.ShapeDtypeStruct((NB, TILE, D), BF),
        grid_spec=pltpu.PrefetchScalarGridSpec(
            num_scalar_prefetch=3,
            grid=(NB,),
            in_specs=[
                pl.BlockSpec((1, TILE, D), lambda b, *_: (b, 0, 0)),
                pl.BlockSpec((NT, TILE, D), lambda b, *_: (b, 0, 0)),
                weight,
                weight,
                weight,
                weight,
                wide,
                wide,
            ],
            out_specs=pl.BlockSpec((1, TILE, D), lambda b, *_: (b, 0, 0)),
            scratch_shapes=[
                pltpu.VMEM((NT * TILE, D), BF),
                pltpu.VMEM((NT * TILE, D), BF),
                pltpu.VMEM((TILE, D), F32),
                pltpu.VMEM((NREL, STRIPS, WIN), BF),
                pltpu.VMEM((NREL, STRIPS, WIN), BF),
            ],
        ),
        compiler_params=pltpu.CompilerParams(vmem_limit_bytes=60 << 20),
    )(table, prior, gate, blocks, fetched, wq, wk, wv, wo, att, msg)


def contrast_kernel(
    tab, weight, emb, pos, loss, mean, offer, negs, part, lanes, doms, ss, rs, sl, rl, sd, rd
):
    y = lax.axis_index("dom_0")
    core = lax.axis_index("dom_1")
    z = lax.axis_index("narrow_0")
    x = lax.axis_index("narrow_1")
    lane = z * RING + x
    dom = y * 2 + core

    def lane_id(by):
        other = (lane + by) % LANES
        return {"narrow_0": other // RING, "narrow_1": other % RING}

    def dom_id(by):
        other = (dom + by) % 8
        return {"dom_0": other // 2, "dom_1": other % 2}

    barrier = pltpu.get_barrier_semaphore()
    for by in range(1, LANES):
        pl.semaphore_signal(barrier, 1, device_id=lane_id(by), device_id_type=MESH)
    for by in range(1, 8):
        pl.semaphore_signal(barrier, 1, device_id=dom_id(by), device_id_type=MESH)
    pl.semaphore_wait(barrier, LANES - 1 + 7)

    def give(s):
        return pltpu.make_async_remote_copy(
            src_ref=offer.at[s],
            dst_ref=negs.at[s],
            send_sem=ss.at[s],
            recv_sem=rs.at[s],
            device_id=lane_id(s + 1),
            device_id_type=MESH,
        )

    for s in range(STEPS):
        offer[s] = emb[tab[SCHED + s]]
        give(s).start()
    for s in range(STEPS):
        give(s).wait_recv()

    inv = 1.0 / math.sqrt(D)
    total = jnp.zeros((1, TILE), F32)
    for b in range(NB):
        own = emb[b]
        tb = tab[OTYPE + b]
        prod = own.astype(F32) * pos[b].astype(F32)
        fold = prod[:, 0:TILE]
        for c in range(1, D // TILE):
            fold = fold + prod[:, c * TILE : (c + 1) * TILE]
        positive = jnp.sum(fold.T, axis=0, keepdims=True) * inv
        logits = []
        high = positive
        for s in range(STEPS):
            v = dot_t(negs[s], own) * inv
            v = jnp.where(tab[NTYP + s] == tb, v, -jnp.inf)
            high = jnp.maximum(high, jnp.max(v, axis=0, keepdims=True))
            logits.append(v)
        den = jnp.exp(positive - high)
        for v in logits:
            den = den + jnp.sum(jnp.exp(v - high), axis=0, keepdims=True)
        row = high + jnp.log(den) - positive
        loss[b : b + 1, :] = row
        total = total + row * weight[tb]
    part[...] = jnp.broadcast_to(total, (8, TILE))

    def lane_copy(by):
        return pltpu.make_async_remote_copy(
            src_ref=part,
            dst_ref=lanes.at[by],
            send_sem=sl.at[by],
            recv_sem=rl.at[by],
            device_id=lane_id(by),
            device_id_type=MESH,
        )

    for by in range(1, LANES):
        lane_copy(by).start()
    lanes[0] = part[...]
    for by in range(1, LANES):
        lane_copy(by).wait_recv()
    for by in range(1, LANES):
        lane_copy(by).wait_send()
    acc = lanes[lane]
    for a in range(1, LANES):
        acc = acc + lanes[(lane - a + LANES) % LANES]
    doms[0] = acc

    def dom_copy(by):
        return pltpu.make_async_remote_copy(
            src_ref=doms.at[0],
            dst_ref=doms.at[by],
            send_sem=sd.at[by],
            recv_sem=rd.at[by],
            device_id=dom_id(by),
            device_id_type=MESH,
        )

    for by in range(1, 8):
        dom_copy(by).start()
    for by in range(1, 8):
        dom_copy(by).wait_recv()
    acc = doms[dom]
    for a in range(1, 8):
        acc = acc + doms[(dom - a + 8) % 8]
    whole = jnp.sum(acc, axis=1, keepdims=True) * (1.0 / (NB * TILE * 128))
    mean[...] = jnp.broadcast_to(whole, (8, TILE))
    for by in range(1, 8):
        dom_copy(by).wait_send()
    for s in range(STEPS):
        give(s).wait_send()


def contrast(table, weight, emb, pos):
    smem = pl.BlockSpec(memory_space=pltpu.SMEM)
    vmem = pl.BlockSpec(memory_space=pltpu.VMEM)
    return pl.pallas_call(
        contrast_kernel,
        name="contrast",
        out_shape=(
            jax.ShapeDtypeStruct((NB, TILE), F32),
            jax.ShapeDtypeStruct((8, TILE), F32),
        ),
        in_specs=[smem, smem, vmem, vmem],
        out_specs=(vmem, vmem),
        scratch_shapes=[
            pltpu.VMEM((STEPS, TILE, D), BF),
            pltpu.VMEM((STEPS, TILE, D), BF),
            pltpu.VMEM((8, TILE), F32),
            pltpu.VMEM((LANES, 8, TILE), F32),
            pltpu.VMEM((8, 8, TILE), F32),
            pltpu.SemaphoreType.DMA((STEPS,)),
            pltpu.SemaphoreType.DMA((STEPS,)),
            pltpu.SemaphoreType.DMA((LANES,)),
            pltpu.SemaphoreType.DMA((LANES,)),
            pltpu.SemaphoreType.DMA((8,)),
            pltpu.SemaphoreType.DMA((8,)),
        ],
        compiler_params=pltpu.CompilerParams(
            collective_id=1, has_side_effects=True, vmem_limit_bytes=60 << 20
        ),
    )(table, weight, emb, pos)


def shards(
    feats,
    node_type,
    tiles,
    relation,
    neg_sched,
    w_query,
    w_key,
    w_value,
    w_out,
    rel_att,
    rel_msg,
    rel_prior,
    skip_gate,
    pos_view,
    type_weight,
):
    table = prep(tiles, node_type, relation, neg_sched)
    blocks = feats.reshape(NB, TILE, D)
    fetched = exchange(table, blocks)
    emb = attend(
        table,
        rel_prior.reshape(-1),
        skip_gate,
        blocks,
        fetched,
        w_query,
        w_key,
        w_value,
        w_out,
        rel_att.reshape(NREL, D, DH),
        rel_msg.reshape(NREL, D, DH),
    )
    loss, mean = contrast(table, type_weight, emb, pos_view.reshape(NB, TILE, D))
    return emb.reshape(NB * TILE, D), loss.reshape(NB * TILE), mean[0, 0]


def solution(mesh):
    finer = Mesh(mesh.devices.reshape(4, 2, 4, 4), DOM_NARROW)
    in_specs = (
        P(DOM_NARROW, None),
        P(DOM),
        P(DOM, None),
        P(DOM_NARROW, None),
        P(DOM, None),
        P(),
        P(),
        P(),
        P(),
        P(),
        P(),
        P(),
        P(),
        P(DOM_NARROW, None),
        P(),
    )
    out_specs = (P(DOM_NARROW, None), P(DOM_NARROW), P())
    return jax.shard_map(
        shards, mesh=finer, in_specs=in_specs, out_specs=out_specs, check_vma=False
    )
```

```python
import functools
import math

import jax
import jax.numpy as jnp
from jax import lax
from jax.experimental import pallas as pl
from jax.experimental.pallas import tpu as pltpu
from jax.sharding import Mesh
from jax.sharding import PartitionSpec as P

D = 768
HEADS = 8
DH = 96
TILE = 128
HALF = TILE // 2
NT = 4
NB = 8
REQ = NB * NT
RING = 4
CAP = 3
NREL = 5
STEPS = 8
LANES = 16
WIN = 256
STRIP = [(0, 384), (128, 640), (384, 768)]
DOM_NARROW = ("dom_0", "dom_1", "narrow_0", "narrow_1")
DOM = ("dom_0", "dom_1")
MESH = pl.DeviceIdType.MESH
BF = jnp.bfloat16
F32 = jnp.float32

SEL = 0
IDX = 72
STYPE = 136
RELA = 168
PLACE = 200
ORDER = 232
STAGE = 264
OTYPE = 296
TABLE = 304
READY = [11, 17, 23, 32]
STAGE_OF = {(1, 3): 1, (3, 1): 1, (2, 3): 2, (3, 2): 2, (1, 2): 3, (2, 1): 3, (2, 2): 3}
STRIP_AT = [0, 384, 896]
STRIPS = 1280
PAIR = [0, 128, 384, 512]


def dot(a, b):
    return jnp.dot(a, b, preferred_element_type=F32)


def dot_t(a, b):
    return lax.dot_general(a, b, (((1,), (1,)), ((), ())), preferred_element_type=F32)


def head_of(index):
    return sum((index >= DH * h).astype(jnp.int32) for h in range(1, HEADS))


def widen(rel, wide):
    for c, (lo, hi) in enumerate(STRIP):
        col = lax.broadcasted_iota(jnp.int32, (DH, WIN), 1) + c * WIN
        row = lax.broadcasted_iota(jnp.int32, (DH, WIN), 0)
        place = (col - DH * head_of(col) == row).astype(F32).astype(BF)
        full = dot(rel[lo:hi, :], place)
        col = lax.broadcasted_iota(jnp.int32, (hi - lo, WIN), 1) + c * WIN
        row = lax.broadcasted_iota(jnp.int32, (hi - lo, WIN), 0) + lo
        full = jnp.where(head_of(row) == head_of(col), full, 0.0)
        wide[STRIP_AT[c] : STRIP_AT[c] + hi - lo, :] = full.astype(BF)


def spread(rows, wide):
    return jnp.concatenate(
        [
            dot(rows[:, lo:hi], wide[STRIP_AT[c] : STRIP_AT[c] + hi - lo, :])
            for c, (lo, hi) in enumerate(STRIP)
        ],
        axis=1,
    )


def layer_kernel(
    tiles, types, relation, prior, gate, feats, wq, wk, wv, wo, att, msg,
    out,
    tab, near0, near1, near2, near3, far, held, send, transit,
    wqo, wks, wvs, raw, att_wide, msg_wide, turned, keyed, message, pairs, agg,
    lsem, wsem, esem, s1, r1, s2, r2,
):
    z = lax.axis_index("narrow_0")
    x = lax.axis_index("narrow_1")
    lane = z * RING + x
    coord = [x, z]
    name = ["narrow_1", "narrow_0"]
    near = [near0, near1, near2, near3]

    def to(axis, by):
        return {name[axis]: (coord[axis] + by) % RING}

    local = [
        pltpu.make_async_copy(feats.at[:, pl.ds(rt * HALF, HALF), :], near0.at[rt], lsem.at[rt])
        for rt in range(2)
    ]
    for c in local:
        c.start()
    barrier = pltpu.get_barrier_semaphore()
    for axis in range(2):
        for by in (1, 3):
            pl.semaphore_signal(barrier, 1, device_id=to(axis, by), device_id_type=MESH)
    pl.semaphore_wait(barrier, 4)
    for c in local:
        c.wait()

    def first(rt, way, part):
        by = slot = (1, 3)[way]
        half = part if way == 0 else 1 - part
        return pltpu.make_async_remote_copy(
            src_ref=near0.at[rt, pl.ds(half * 4, 4)],
            dst_ref=near[slot].at[rt, pl.ds(half * 4, 4)],
            send_sem=s1.at[rt, way, part],
            recv_sem=r1.at[rt, way, part],
            device_id=to(rt, by),
            device_id_type=MESH,
        )

    def forward(rt, way):
        by = slot = (1, 3)[way]
        return pltpu.make_async_remote_copy(
            src_ref=near[slot].at[rt, pl.ds(way * 4, 4)],
            dst_ref=near2.at[rt, pl.ds(way * 4, 4)],
            send_sem=s1.at[rt, way, 2],
            recv_sem=r1.at[rt, way, 2],
            device_id=to(rt, by),
            device_id_type=MESH,
        )

    def second(rt, d, o):
        at = pl.ds((d - 1) * 12 + o * CAP, CAP)
        if d == 2:
            dst = transit.at[rt, pl.ds(o * CAP, CAP)]
            by = 1 if o < 2 else 3
        else:
            dst = far.at[rt, at]
            by = d
        return pltpu.make_async_remote_copy(
            src_ref=send.at[rt, at],
            dst_ref=dst,
            send_sem=s2.at[rt, d - 1, o],
            recv_sem=r2.at[rt, d - 1, o],
            device_id=to(1 - rt, by),
            device_id_type=MESH,
        )

    def onward(rt, o):
        return pltpu.make_async_remote_copy(
            src_ref=transit.at[rt, pl.ds(o * CAP, CAP)],
            dst_ref=far.at[rt, pl.ds(12 + o * CAP, CAP)],
            send_sem=s2.at[rt, 3, o],
            recv_sem=r2.at[rt, 3, o],
            device_id=to(1 - rt, 1 if o < 2 else 3),
            device_id_type=MESH,
        )

    def pick(o):
        for d in (2, 1, 3):
            for rt in range(2):
                for k in range(CAP):
                    at = (d - 1) * 12 + o * CAP + k
                    send[rt, at] = near[o][rt, tab[SEL + rt * 36 + at]]
                second(rt, d, o).start()

    def take(d, o):
        at = (d - 1) * 12 + o * CAP
        for rt in range(2):
            (onward(rt, o) if d == 2 else second(rt, d, o)).wait_recv()
            held[rt, at : at + CAP] = far[rt, at : at + CAP]

    def relay(o):
        for rt in range(2):
            second(rt, 2, o).wait_recv()
            onward(rt, o).start()

    for part in range(2):
        for rt in range(2):
            for way in range(2):
                first(rt, way, part).start()
    load_wq = pltpu.make_async_copy(wq, wqo, wsem.at[0])
    load_wk = pltpu.make_async_copy(wk, wks, wsem.at[1])
    load_wv = pltpu.make_async_copy(wv, wvs, wsem.at[2])
    load_att = pltpu.make_async_copy(att, raw, wsem.at[3])
    load_msg = pltpu.make_async_copy(msg, raw, wsem.at[4])
    load_wo = pltpu.make_async_copy(wo, wqo, wsem.at[5])
    load_att.start()
    load_wq.start()
    load_wk.start()
    load_wv.start()

    for rt in range(2):
        for d in range(1, RING):
            if rt == 0:
                dst = (z + d) % RING * RING + x
            else:
                dst = z * RING + (x + d) % RING

            def ask(p, c, rt=rt, dst=dst):
                c = list(c)
                t = tiles[p % NT, dst * NB + p // NT]
                owner = t // NB
                oz = (z - owner // RING + RING) % RING
                ox = (x - owner % RING + RING) % RING
                here, o = (oz, ox) if rt == 0 else (ox, oz)
                for i in range(RING):
                    hit = jnp.logical_and(here == 0, o == i)
                    c[i] = jnp.where(hit, c[i] + c[RING + i] * (t % NB), c[i])
                    c[RING + i] = jnp.where(hit, c[RING + i] * NB, c[RING + i])
                return tuple(c)

            got = lax.fori_loop(
                0, REQ, ask, (jnp.int32(0),) * RING + (jnp.int32(1),) * RING
            )
            for o in range(RING):
                for k in range(CAP):
                    tab[SEL + rt * 36 + (d - 1) * 12 + o * CAP + k] = (
                        got[o] // NB**k
                    ) % NB
    pick(0)

    def mine(p, c):
        c = list(c)
        t = tiles[p % NT, lane * NB + p // NT]
        owner = t // NB
        oz = (z - owner // RING + RING) % RING
        ox = (x - owner % RING + RING) % RING
        back = oz * RING + ox
        k = jnp.int32(0)
        for i in range(LANES):
            hit = back == i
            k = jnp.where(hit, c[i], k)
            c[i] = jnp.where(hit, c[i] + 1, c[i])
        stage = jnp.int32(0)
        for (a, b), v in STAGE_OF.items():
            stage = jnp.where(back == a * RING + b, v, stage)
        tab[IDX + p] = jnp.where(
            oz == 0, ox * NB + t % NB, 32 + (oz - 1) * 12 + ox * CAP + k
        )
        tab[IDX + REQ + p] = jnp.where(
            ox == 0, oz * NB + t % NB, 32 + (ox - 1) * 12 + oz * CAP + k
        )
        tab[STYPE + p] = types[t]
        tab[RELA + p] = relation[p % NT, p // NT]
        tab[STAGE + p] = stage
        for v in range(3):
            c[LANES + v] = c[LANES + v] + jnp.where(stage <= v, 1, 0)
        return tuple(c)

    counts = lax.fori_loop(0, REQ, mine, (jnp.int32(0),) * (LANES + 3))[LANES:]

    def turn(p, c):
        c = list(c)
        stage = tab[STAGE + p]
        place = jnp.int32(0)
        for v in range(4):
            hit = stage == v
            place = jnp.where(hit, c[v], place)
            c[v] = jnp.where(hit, c[v] + 1, c[v])
        tab[PLACE + p] = place
        return tuple(c)

    lax.fori_loop(0, REQ, turn, (jnp.int32(0),) + tuple(counts))

    def invert(n, c):
        found = jnp.int32(0)
        for p in range(REQ):
            found = jnp.where(tab[PLACE + p] == n, p, found)
        tab[ORDER + n] = found
        return c

    lax.fori_loop(0, REQ, invert, 0)
    for b in range(NB):
        tab[OTYPE + b] = types[lane * NB + b]
    pairs[...] = jnp.zeros_like(pairs)

    def widen_all(wide):
        def body(r, c):
            widen(raw.at[r], wide.at[r])
            return c

        lax.fori_loop(0, NREL, body, 0)

    load_att.wait()
    widen_all(att_wide)
    load_msg.start()
    for rt in range(2):
        for way in range(2):
            first(rt, way, 0).wait_recv()
            forward(rt, way).start()

    load_wq.wait()

    def ask_query(b, c):
        rows = jnp.concatenate([near0[0, b], near0[1, b]], axis=0)
        turned[b] = dot(rows, wqo[tab[OTYPE + b]]).astype(BF).T
        return c

    lax.fori_loop(0, NB, ask_query, 0)
    load_wo.start()
    load_msg.wait()
    widen_all(msg_wide)
    load_wk.wait()
    load_wv.wait()
    relay(0)
    for rt in range(2):
        for way in range(2):
            first(rt, way, 1).wait_recv()
    pick(1)
    pick(3)
    for rt in range(2):
        for way in range(2):
            forward(rt, way).wait_recv()
    pick(2)

    def part_of(rt, i):
        rows = held[rt, jnp.clip(i - 32, 0, 35)]
        for o in range(RING):
            rows = jnp.where(i // NB == o, near[o][rt, jnp.clip(i - o * NB, 0, NB - 1)], rows)
        return rows

    def transform(n, c):
        p = tab[ORDER + n]
        src = jnp.concatenate(
            [part_of(0, tab[IDX + p]), part_of(1, tab[IDX + REQ + p])], axis=0
        )
        ts = tab[STYPE + p]
        r = tab[RELA + p]
        key = dot(src, wks[ts]).astype(BF)
        keyed[n] = spread(key, att_wide.at[r]).astype(BF)
        value = dot(src, wvs[ts]).astype(BF)
        message[n] = spread(value, msg_wide.at[r]).astype(BF).T
        return c

    for d, o in ((3, 0), (1, 0), (2, 0), (3, 1)):
        take(d, o)
    relay(3)
    take(3, 3)
    relay(1)
    take(1, 1)
    lax.fori_loop(0, READY[0], transform, 0)
    relay(2)
    take(1, 3)
    lax.fori_loop(READY[0], READY[1], transform, 0)
    take(3, 2)
    take(2, 3)
    lax.fori_loop(READY[1], READY[2], transform, 0)
    take(1, 2)
    take(2, 1)
    take(2, 2)
    lax.fori_loop(READY[2], READY[3], transform, 0)

    for rt in range(2):
        for way in range(2):
            for part in range(2):
                first(rt, way, part).wait_send()
            forward(rt, way).wait_send()
        for o in range(4):
            for d in (1, 2, 3):
                second(rt, d, o).wait_send()
            onward(rt, o).wait_send()
    load_wo.wait()

    left = lax.broadcasted_iota(jnp.int32, (1, WIN), 1) < TILE
    unit = math.log2(math.e) / math.sqrt(DH)

    def attend(b, c):
        where = [tab[PLACE + b * NT + j] for j in range(NT)]
        rel = [tab[RELA + b * NT + j] for j in range(NT)]
        for h in range(HEADS):
            lo = h * DH - PAIR[h // 2]
            pairs[h // 2, lo : lo + DH, h % 2 * TILE : (h % 2 + 1) * TILE] = turned[
                b, h * DH : (h + 1) * DH, :
            ]
        for q in range(HEADS // 2):
            w = PAIR[q]
            scores = []
            for j in range(NT):
                scale = jnp.where(left, prior[rel[j], 2 * q], prior[rel[j], 2 * q + 1]) * unit
                scores.append(dot(keyed[where[j], :, w : w + WIN], pairs[q]) * scale)
            top = jnp.maximum(
                jnp.maximum(scores[0], scores[1]), jnp.maximum(scores[2], scores[3])
            )
            top = jnp.max(top, axis=0, keepdims=True)
            weights = [jnp.exp2(s - top) for s in scores]
            total = jnp.sum(
                (weights[0] + weights[1]) + (weights[2] + weights[3]), axis=0, keepdims=True
            )
            inv = 1.0 / total
            rows = slice(2 * q * DH, (2 * q + 2) * DH)
            lhs = jnp.concatenate([message[where[j], rows, :] for j in range(NT)], axis=1)
            got = dot(lhs, jnp.concatenate([e.astype(BF) for e in weights], axis=0))
            agg[2 * q * DH : (2 * q + 1) * DH, :] = got[:DH, :TILE] * inv[:, :TILE]
            agg[(2 * q + 1) * DH : (2 * q + 2) * DH, :] = got[DH:, TILE:] * inv[:, TILE:]
        merged = agg[...]
        active = (0.5 * merged * (1.0 + lax.erf(merged * math.sqrt(0.5)))).astype(BF).T
        tb = tab[OTYPE + b]
        projected = dot(active, wqo[tb])
        a = jax.nn.sigmoid(jnp.full((1, D), gate[tb], F32))
        for rt in range(2):
            at = slice(rt * HALF, (rt + 1) * HALF)
            own = near0[rt, b].astype(F32)
            send[rt, b] = (a * projected[at] + (1.0 - a) * own).astype(BF)
        return c

    lax.fori_loop(0, NB, attend, 0)
    done = [
        pltpu.make_async_copy(
            send.at[rt, pl.ds(0, NB)], out.at[:, pl.ds(rt * HALF, HALF), :], esem.at[rt]
        )
        for rt in range(2)
    ]
    for c in done:
        c.start()
    for c in done:
        c.wait()


def layer(tiles, types, relation, prior, gate, feats, wq, wk, wv, wo, att, msg):
    smem = pl.BlockSpec(memory_space=pltpu.SMEM)
    hbm = pl.BlockSpec(memory_space=pl.ANY)
    return pl.pallas_call(
        layer_kernel,
        name="layer",
        out_shape=jax.ShapeDtypeStruct((NB, TILE, D), BF),
        in_specs=[smem] * 5 + [hbm] * 7,
        out_specs=hbm,
        scratch_shapes=[
            pltpu.SMEM((TABLE,), jnp.int32),
            *[pltpu.VMEM((2, NB, HALF, D), BF)] * 4,
            pltpu.VMEM((2, 36, HALF, D), BF),
            pltpu.VMEM((2, 36, HALF, D), BF),
            pltpu.VMEM((2, 36, HALF, D), BF),
            pltpu.VMEM((2, 12, HALF, D), BF),
            pltpu.VMEM((3, D, D), BF),
            pltpu.VMEM((3, D, D), BF),
            pltpu.VMEM((3, D, D), BF),
            pltpu.VMEM((NREL, D, DH), BF),
            pltpu.VMEM((NREL, STRIPS, WIN), BF),
            pltpu.VMEM((NREL, STRIPS, WIN), BF),
            pltpu.VMEM((NB, D, TILE), BF),
            pltpu.VMEM((REQ, TILE, D), BF),
            pltpu.VMEM((REQ, D, TILE), BF),
            pltpu.VMEM((HEADS // 2, WIN, WIN), BF),
            pltpu.VMEM((D, TILE), F32),
            pltpu.SemaphoreType.DMA((2,)),
            pltpu.SemaphoreType.DMA((6,)),
            pltpu.SemaphoreType.DMA((2,)),
            pltpu.SemaphoreType.DMA((2, 2, 3)),
            pltpu.SemaphoreType.DMA((2, 2, 3)),
            pltpu.SemaphoreType.DMA((2, 4, 4)),
            pltpu.SemaphoreType.DMA((2, 4, 4)),
        ],
        compiler_params=pltpu.CompilerParams(
            collective_id=0, has_side_effects=True, vmem_limit_bytes=67043328
        ),
    )(tiles, types, relation, prior, gate, feats, wq, wk, wv, wo, att, msg)


def contrast_kernel(
    types, sched, weight, emb, pos, loss, mean, offer, negs, part, lanes, doms, ss, rs, sl, rl, sd, rd
):
    y = lax.axis_index("dom_0")
    core = lax.axis_index("dom_1")
    z = lax.axis_index("narrow_0")
    x = lax.axis_index("narrow_1")
    lane = z * RING + x
    dom = y * 2 + core

    def lane_id(by):
        other = (lane + by) % LANES
        return {"narrow_0": other // RING, "narrow_1": other % RING}

    def dom_id(by):
        other = (dom + by) % 8
        return {"dom_0": other // 2, "dom_1": other % 2}

    barrier = pltpu.get_barrier_semaphore()
    for by in range(1, LANES):
        pl.semaphore_signal(barrier, 1, device_id=lane_id(by), device_id_type=MESH)
    for by in range(1, 8):
        pl.semaphore_signal(barrier, 1, device_id=dom_id(by), device_id_type=MESH)
    pl.semaphore_wait(barrier, LANES - 1 + 7)

    def give(s):
        return pltpu.make_async_remote_copy(
            src_ref=offer.at[s],
            dst_ref=negs.at[s],
            send_sem=ss.at[s],
            recv_sem=rs.at[s],
            device_id=lane_id(s + 1),
            device_id_type=MESH,
        )

    for s in range(STEPS):
        offer[s] = emb[sched[s, lane]]
        give(s).start()
    for s in range(STEPS):
        give(s).wait_recv()

    inv = 1.0 / math.sqrt(D)
    kinds = []
    for s in range(STEPS):
        frm = (lane + LANES - s - 1) % LANES
        kinds.append(types[frm * NB + sched[s, frm]])
    total = jnp.zeros((1, TILE), F32)
    for b in range(NB):
        own = emb[b]
        tb = types[lane * NB + b]
        prod = own.astype(F32) * pos[b].astype(F32)
        fold = prod[:, 0:TILE]
        for c in range(1, D // TILE):
            fold = fold + prod[:, c * TILE : (c + 1) * TILE]
        positive = jnp.sum(fold.T, axis=0, keepdims=True) * inv
        logits = []
        high = positive
        for s in range(STEPS):
            v = dot_t(negs[s], own) * inv
            v = jnp.where(kinds[s] == tb, v, -jnp.inf)
            high = jnp.maximum(high, jnp.max(v, axis=0, keepdims=True))
            logits.append(v)
        den = jnp.exp(positive - high)
        for v in logits:
            den = den + jnp.sum(jnp.exp(v - high), axis=0, keepdims=True)
        row = high + jnp.log(den) - positive
        loss[b : b + 1, :] = row
        total = total + row * weight[tb]
    part[...] = jnp.broadcast_to(total, (8, TILE))

    def lane_copy(by):
        return pltpu.make_async_remote_copy(
            src_ref=part,
            dst_ref=lanes.at[by],
            send_sem=sl.at[by],
            recv_sem=rl.at[by],
            device_id=lane_id(by),
            device_id_type=MESH,
        )

    for by in range(1, LANES):
        lane_copy(by).start()
    lanes[0] = part[...]
    for by in range(1, LANES):
        lane_copy(by).wait_recv()
    for by in range(1, LANES):
        lane_copy(by).wait_send()
    acc = lanes[lane]
    for a in range(1, LANES):
        acc = acc + lanes[(lane - a + LANES) % LANES]
    doms[0] = acc

    def dom_copy(by):
        return pltpu.make_async_remote_copy(
            src_ref=doms.at[0],
            dst_ref=doms.at[by],
            send_sem=sd.at[by],
            recv_sem=rd.at[by],
            device_id=dom_id(by),
            device_id_type=MESH,
        )

    for by in range(1, 8):
        dom_copy(by).start()
    for by in range(1, 8):
        dom_copy(by).wait_recv()
    acc = doms[dom]
    for a in range(1, 8):
        acc = acc + doms[(dom - a + 8) % 8]
    whole = jnp.sum(acc, axis=1, keepdims=True) * (1.0 / (NB * TILE * 128))
    mean[...] = jnp.broadcast_to(whole, (8, TILE))
    for by in range(1, 8):
        dom_copy(by).wait_send()
    for s in range(STEPS):
        give(s).wait_send()


def contrast(types, sched, weight, emb, pos):
    smem = pl.BlockSpec(memory_space=pltpu.SMEM)
    vmem = pl.BlockSpec(memory_space=pltpu.VMEM)
    return pl.pallas_call(
        contrast_kernel,
        name="contrast",
        out_shape=(
            jax.ShapeDtypeStruct((NB, TILE), F32),
            jax.ShapeDtypeStruct((8, TILE), F32),
        ),
        in_specs=[smem, smem, smem, vmem, vmem],
        out_specs=(vmem, vmem),
        scratch_shapes=[
            pltpu.VMEM((STEPS, TILE, D), BF),
            pltpu.VMEM((STEPS, TILE, D), BF),
            pltpu.VMEM((8, TILE), F32),
            pltpu.VMEM((LANES, 8, TILE), F32),
            pltpu.VMEM((8, 8, TILE), F32),
            pltpu.SemaphoreType.DMA((STEPS,)),
            pltpu.SemaphoreType.DMA((STEPS,)),
            pltpu.SemaphoreType.DMA((LANES,)),
            pltpu.SemaphoreType.DMA((LANES,)),
            pltpu.SemaphoreType.DMA((8,)),
            pltpu.SemaphoreType.DMA((8,)),
        ],
        compiler_params=pltpu.CompilerParams(
            collective_id=1, has_side_effects=True, vmem_limit_bytes=60 << 20
        ),
    )(types, sched, weight, emb, pos)


def shards(
    feats,
    node_type,
    tiles,
    relation,
    neg_sched,
    w_query,
    w_key,
    w_value,
    w_out,
    rel_att,
    rel_msg,
    rel_prior,
    skip_gate,
    pos_view,
    type_weight,
):
    blocks = feats.reshape(NB, TILE, D)
    emb = layer(
        tiles.T,
        node_type,
        relation.T,
        rel_prior,
        skip_gate,
        blocks,
        w_query,
        w_key,
        w_value,
        w_out,
        rel_att.reshape(NREL, D, DH),
        rel_msg.reshape(NREL, D, DH),
    )
    loss, mean = contrast(
        node_type, neg_sched.T, type_weight, emb, pos_view.reshape(NB, TILE, D)
    )
    return emb.reshape(NB * TILE, D), loss.reshape(NB * TILE), mean[0, 0]


def solution(mesh):
    finer = Mesh(mesh.devices.reshape(4, 2, 4, 4), DOM_NARROW)
    in_specs = (
        P(DOM_NARROW, None),
        P(DOM),
        P(DOM, None),
        P(DOM_NARROW, None),
        P(DOM, None),
        P(),
        P(),
        P(),
        P(),
        P(),
        P(),
        P(),
        P(),
        P(DOM_NARROW, None),
        P(),
    )
    out_specs = (P(DOM_NARROW, None), P(DOM_NARROW), P())
    return jax.shard_map(
        shards, mesh=finer, in_specs=in_specs, out_specs=out_specs, check_vma=False
    )
```

```python
import functools
import math

import jax
import jax.numpy as jnp
from jax import lax
from jax.experimental import pallas as pl
from jax.experimental.pallas import tpu as pltpu
from jax.sharding import Mesh
from jax.sharding import PartitionSpec as P

D = 768
HEADS = 8
DH = 96
TILE = 128
HALF = TILE // 2
NT = 4
NB = 8
REQ = NB * NT
RING = 4
CAP = 3
NREL = 5
STEPS = 8
LANES = 16
WIN = 256
STRIP = [(0, 384), (128, 640), (384, 768)]
DOM_NARROW = ("dom_0", "dom_1", "narrow_0", "narrow_1")
DOM = ("dom_0", "dom_1")
MESH = pl.DeviceIdType.MESH
BF = jnp.bfloat16
F32 = jnp.float32

SEL = 0
IDX = 72
STYPE = 136
RELA = 168
PLACE = 200
ORDER = 232
STAGE = 264
OTYPE = 296
FIRST = 304
TURN = 312
BLOCK = 320
TABLE = 328
READY = [11, 17, 23, 32]
STAGE_OF = {(1, 3): 1, (3, 1): 1, (2, 3): 2, (3, 2): 2, (1, 2): 3, (2, 1): 3, (2, 2): 3}
STRIP_AT = [0, 384, 896]
STRIPS = 1280
PAIR = [0, 128, 384, 512]


def dot(a, b):
    return jnp.dot(a, b, preferred_element_type=F32)


def dot_t(a, b):
    return lax.dot_general(a, b, (((1,), (1,)), ((), ())), preferred_element_type=F32)


def head_of(index):
    return sum((index >= DH * h).astype(jnp.int32) for h in range(1, HEADS))


def widen(rel, wide):
    for c, (lo, hi) in enumerate(STRIP):
        col = lax.broadcasted_iota(jnp.int32, (DH, WIN), 1) + c * WIN
        row = lax.broadcasted_iota(jnp.int32, (DH, WIN), 0)
        place = (col - DH * head_of(col) == row).astype(F32).astype(BF)
        full = dot(rel[lo:hi, :], place)
        col = lax.broadcasted_iota(jnp.int32, (hi - lo, WIN), 1) + c * WIN
        row = lax.broadcasted_iota(jnp.int32, (hi - lo, WIN), 0) + lo
        full = jnp.where(head_of(row) == head_of(col), full, 0.0)
        wide[STRIP_AT[c] : STRIP_AT[c] + hi - lo, :] = full.astype(BF)


def spread(rows, wide):
    return jnp.concatenate(
        [
            dot(rows[:, lo:hi], wide[STRIP_AT[c] : STRIP_AT[c] + hi - lo, :])
            for c, (lo, hi) in enumerate(STRIP)
        ],
        axis=1,
    )


def layer_kernel(
    tiles, types, relation, sched, prior, gate, weight, feats, pos, wq, wk, wv, wo, att, msg,
    out, loss, mean,
    tab, near0, near1, near2, near3, far, held, send, transit,
    wqo, wks, wvs, raw, att_wide, msg_wide, turned, keyed, message, pairs, agg,
    negs, via, positive, rows_of, subtotal, lanes, doms,
    lsem, wsem, esem, s1, r1, s2, r2, s3, r3, sl, rl, sd, rd,
):
    z = lax.axis_index("narrow_0")
    x = lax.axis_index("narrow_1")
    lane = z * RING + x
    coord = [x, z]
    name = ["narrow_1", "narrow_0"]
    near = [near0, near1, near2, near3]

    def to(axis, by):
        return {name[axis]: (coord[axis] + by) % RING}

    local = [
        pltpu.make_async_copy(feats.at[:, pl.ds(rt * HALF, HALF), :], near0.at[rt], lsem.at[rt])
        for rt in range(2)
    ]
    for c in local:
        c.start()
    dom = lax.axis_index("dom_0") * 2 + lax.axis_index("dom_1")

    def lane_id(by):
        other = (lane + by) % LANES
        return {"narrow_0": other // RING, "narrow_1": other % RING}

    def dom_id(by):
        other = (dom + by) % 8
        return {"dom_0": other // 2, "dom_1": other % 2}

    barrier = pltpu.get_barrier_semaphore()
    for by in range(1, LANES):
        pl.semaphore_signal(barrier, 1, device_id=lane_id(by), device_id_type=MESH)
    for by in range(1, 8):
        pl.semaphore_signal(barrier, 1, device_id=dom_id(by), device_id_type=MESH)
    pl.semaphore_wait(barrier, LANES - 1 + 7)
    for c in local:
        c.wait()

    def first(rt, way, part):
        by = slot = (1, 3)[way]
        half = part if way == 0 else 1 - part
        return pltpu.make_async_remote_copy(
            src_ref=near0.at[rt, pl.ds(half * 4, 4)],
            dst_ref=near[slot].at[rt, pl.ds(half * 4, 4)],
            send_sem=s1.at[rt, way, part],
            recv_sem=r1.at[rt, way, part],
            device_id=to(rt, by),
            device_id_type=MESH,
        )

    def forward(rt, way):
        by = slot = (1, 3)[way]
        return pltpu.make_async_remote_copy(
            src_ref=near[slot].at[rt, pl.ds(way * 4, 4)],
            dst_ref=near2.at[rt, pl.ds(way * 4, 4)],
            send_sem=s1.at[rt, way, 2],
            recv_sem=r1.at[rt, way, 2],
            device_id=to(rt, by),
            device_id_type=MESH,
        )

    def second(rt, d, o):
        at = pl.ds((d - 1) * 12 + o * CAP, CAP)
        if d == 2:
            dst = transit.at[rt, pl.ds(o * CAP, CAP)]
            by = 1 if o < 2 else 3
        else:
            dst = far.at[rt, at]
            by = d
        return pltpu.make_async_remote_copy(
            src_ref=send.at[rt, at],
            dst_ref=dst,
            send_sem=s2.at[rt, d - 1, o],
            recv_sem=r2.at[rt, d - 1, o],
            device_id=to(1 - rt, by),
            device_id_type=MESH,
        )

    def onward(rt, o):
        return pltpu.make_async_remote_copy(
            src_ref=transit.at[rt, pl.ds(o * CAP, CAP)],
            dst_ref=far.at[rt, pl.ds(12 + o * CAP, CAP)],
            send_sem=s2.at[rt, 3, o],
            recv_sem=r2.at[rt, 3, o],
            device_id=to(1 - rt, 1 if o < 2 else 3),
            device_id_type=MESH,
        )

    def pick(o):
        for d in (2, 1, 3):
            for rt in range(2):
                for k in range(CAP):
                    at = (d - 1) * 12 + o * CAP + k
                    send[rt, at] = near[o][rt, tab[SEL + rt * 36 + at]]
                second(rt, d, o).start()

    def take(d, o):
        at = (d - 1) * 12 + o * CAP
        for rt in range(2):
            (onward(rt, o) if d == 2 else second(rt, d, o)).wait_recv()
            held[rt, at : at + CAP] = far[rt, at : at + CAP]

    def relay(o):
        for rt in range(2):
            second(rt, 2, o).wait_recv()
            onward(rt, o).start()

    for part in range(2):
        for rt in range(2):
            for way in range(2):
                first(rt, way, part).start()
    load_wq = pltpu.make_async_copy(wq, wqo, wsem.at[0])
    load_wk = pltpu.make_async_copy(wk, wks, wsem.at[1])
    load_wv = pltpu.make_async_copy(wv, wvs, wsem.at[2])
    load_att = pltpu.make_async_copy(att, raw, wsem.at[3])
    load_msg = pltpu.make_async_copy(msg, raw, wsem.at[4])
    load_wo = pltpu.make_async_copy(wo, wqo, wsem.at[5])
    load_att.start()
    load_wq.start()
    load_wk.start()
    load_wv.start()

    for rt in range(2):
        for d in range(1, RING):
            if rt == 0:
                dst = (z + d) % RING * RING + x
            else:
                dst = z * RING + (x + d) % RING

            def ask(p, c, rt=rt, dst=dst):
                c = list(c)
                t = tiles[p % NT, dst * NB + p // NT]
                owner = t // NB
                oz = (z - owner // RING + RING) % RING
                ox = (x - owner % RING + RING) % RING
                here, o = (oz, ox) if rt == 0 else (ox, oz)
                for i in range(RING):
                    hit = jnp.logical_and(here == 0, o == i)
                    c[i] = jnp.where(hit, c[i] + c[RING + i] * (t % NB), c[i])
                    c[RING + i] = jnp.where(hit, c[RING + i] * NB, c[RING + i])
                return tuple(c)

            got = lax.fori_loop(
                0, REQ, ask, (jnp.int32(0),) * RING + (jnp.int32(1),) * RING
            )
            for o in range(RING):
                for k in range(CAP):
                    tab[SEL + rt * 36 + (d - 1) * 12 + o * CAP + k] = (
                        got[o] // NB**k
                    ) % NB
    pick(0)

    def mine(p, c):
        c = list(c)
        t = tiles[p % NT, lane * NB + p // NT]
        owner = t // NB
        oz = (z - owner // RING + RING) % RING
        ox = (x - owner % RING + RING) % RING
        back = oz * RING + ox
        k = jnp.int32(0)
        for i in range(LANES):
            hit = back == i
            k = jnp.where(hit, c[i], k)
            c[i] = jnp.where(hit, c[i] + 1, c[i])
        stage = jnp.int32(0)
        for (a, b), v in STAGE_OF.items():
            stage = jnp.where(back == a * RING + b, v, stage)
        tab[IDX + p] = jnp.where(
            oz == 0, ox * NB + t % NB, 32 + (oz - 1) * 12 + ox * CAP + k
        )
        tab[IDX + REQ + p] = jnp.where(
            ox == 0, oz * NB + t % NB, 32 + (ox - 1) * 12 + oz * CAP + k
        )
        tab[STYPE + p] = types[t]
        tab[RELA + p] = relation[p % NT, p // NT]
        tab[STAGE + p] = stage
        for v in range(3):
            c[LANES + v] = c[LANES + v] + jnp.where(stage <= v, 1, 0)
        return tuple(c)

    counts = lax.fori_loop(0, REQ, mine, (jnp.int32(0),) * (LANES + 3))[LANES:]

    def turn(p, c):
        c = list(c)
        stage = tab[STAGE + p]
        place = jnp.int32(0)
        for v in range(4):
            hit = stage == v
            place = jnp.where(hit, c[v], place)
            c[v] = jnp.where(hit, c[v] + 1, c[v])
        tab[PLACE + p] = place
        return tuple(c)

    lax.fori_loop(0, REQ, turn, (jnp.int32(0),) + tuple(counts))

    def invert(n, c):
        found = jnp.int32(0)
        for p in range(REQ):
            found = jnp.where(tab[PLACE + p] == n, p, found)
        tab[ORDER + n] = found
        return c

    lax.fori_loop(0, REQ, invert, 0)
    for b in range(NB):
        tab[OTYPE + b] = types[lane * NB + b]
        at = jnp.int32(STEPS + b)
        for n in reversed(range(STEPS)):
            at = jnp.where(sched[STEPS - 1 - n, lane] == b, n, at)
        tab[FIRST + b] = at
    for b in range(NB):
        ahead = jnp.int32(0)
        for e in range(NB):
            ahead = ahead + jnp.where(tab[FIRST + e] < tab[FIRST + b], 1, 0)
        tab[TURN + b] = ahead
    for n in range(NB):
        found = jnp.int32(0)
        for b in range(NB):
            found = jnp.where(tab[TURN + b] == n, b, found)
        tab[BLOCK + n] = found
    pairs[...] = jnp.zeros_like(pairs)

    def widen_all(wide):
        def body(r, c):
            widen(raw.at[r], wide.at[r])
            return c

        lax.fori_loop(0, NREL, body, 0)

    load_att.wait()
    widen_all(att_wide)
    load_msg.start()
    for rt in range(2):
        for way in range(2):
            first(rt, way, 0).wait_recv()
            forward(rt, way).start()

    load_wq.wait()

    def ask_query(n, c):
        b = tab[BLOCK + n]
        rows = jnp.concatenate([near0[0, b], near0[1, b]], axis=0)
        turned[n] = dot(rows, wqo[tab[OTYPE + b]]).astype(BF).T
        return c

    lax.fori_loop(0, NB, ask_query, 0)
    load_wo.start()
    load_msg.wait()
    widen_all(msg_wide)
    load_wk.wait()
    load_wv.wait()
    relay(0)
    for rt in range(2):
        for way in range(2):
            first(rt, way, 1).wait_recv()
    pick(1)
    pick(3)
    for rt in range(2):
        for way in range(2):
            forward(rt, way).wait_recv()
    pick(2)

    def part_of(rt, i):
        rows = held[rt, jnp.clip(i - 32, 0, 35)]
        for o in range(RING):
            rows = jnp.where(i // NB == o, near[o][rt, jnp.clip(i - o * NB, 0, NB - 1)], rows)
        return rows

    def transform(n, c):
        p = tab[ORDER + n]
        src = jnp.concatenate(
            [part_of(0, tab[IDX + p]), part_of(1, tab[IDX + REQ + p])], axis=0
        )
        ts = tab[STYPE + p]
        r = tab[RELA + p]
        key = dot(src, wks[ts]).astype(BF)
        keyed[n] = spread(key, att_wide.at[r]).astype(BF)
        value = dot(src, wvs[ts]).astype(BF)
        message[n] = spread(value, msg_wide.at[r]).astype(BF).T
        return c

    for d, o in ((3, 0), (1, 0), (2, 0), (3, 1)):
        take(d, o)
    relay(3)
    take(3, 3)
    relay(1)
    take(1, 1)
    lax.fori_loop(0, READY[0], transform, 0)
    relay(2)
    take(1, 3)
    lax.fori_loop(READY[0], READY[1], transform, 0)
    take(3, 2)
    take(2, 3)
    lax.fori_loop(READY[1], READY[2], transform, 0)
    take(1, 2)
    take(2, 1)
    take(2, 2)
    lax.fori_loop(READY[2], READY[3], transform, 0)

    for rt in range(2):
        for way in range(2):
            for part in range(2):
                first(rt, way, part).wait_send()
            forward(rt, way).wait_send()
        for o in range(4):
            for d in (1, 2, 3):
                second(rt, d, o).wait_send()
            onward(rt, o).wait_send()
    load_wo.wait()

    load_pos = [
        pltpu.make_async_copy(
            pos.at[:, pl.ds(rt * HALF, HALF), :], far.at[rt, pl.ds(0, NB)], lsem.at[rt]
        )
        for rt in range(2)
    ]
    for c in load_pos:
        c.start()

    left = lax.broadcasted_iota(jnp.int32, (1, WIN), 1) < TILE
    unit = math.log2(math.e) / math.sqrt(DH)

    def attend(n, c):
        b = tab[BLOCK + n]
        where = [tab[PLACE + b * NT + j] for j in range(NT)]
        rel = [tab[RELA + b * NT + j] for j in range(NT)]
        for h in range(HEADS):
            lo = h * DH - PAIR[h // 2]
            pairs[h // 2, lo : lo + DH, h % 2 * TILE : (h % 2 + 1) * TILE] = turned[
                n, h * DH : (h + 1) * DH, :
            ]
        for q in range(HEADS // 2):
            w = PAIR[q]
            scores = []
            for j in range(NT):
                scale = jnp.where(left, prior[rel[j], 2 * q], prior[rel[j], 2 * q + 1]) * unit
                scores.append(dot(keyed[where[j], :, w : w + WIN], pairs[q]) * scale)
            top = jnp.maximum(
                jnp.maximum(scores[0], scores[1]), jnp.maximum(scores[2], scores[3])
            )
            top = jnp.max(top, axis=0, keepdims=True)
            weights = [jnp.exp2(s - top) for s in scores]
            total = jnp.sum(
                (weights[0] + weights[1]) + (weights[2] + weights[3]), axis=0, keepdims=True
            )
            inv = 1.0 / total
            rows = slice(2 * q * DH, (2 * q + 2) * DH)
            lhs = jnp.concatenate([message[where[j], rows, :] for j in range(NT)], axis=1)
            got = dot(lhs, jnp.concatenate([e.astype(BF) for e in weights], axis=0))
            agg[2 * q * DH : (2 * q + 1) * DH, :] = got[:DH, :TILE] * inv[:, :TILE]
            agg[(2 * q + 1) * DH : (2 * q + 2) * DH, :] = got[DH:, TILE:] * inv[:, TILE:]
        merged = agg[...]
        active = (0.5 * merged * (1.0 + lax.erf(merged * math.sqrt(0.5)))).astype(BF).T
        tb = tab[OTYPE + b]
        projected = dot(active, wqo[tb])
        a = jax.nn.sigmoid(jnp.full((1, D), gate[tb], F32))
        own = jnp.concatenate([near0[0, b], near0[1, b]], axis=0).astype(F32)
        emb = (a * projected + (1.0 - a) * own).astype(BF)
        held[0, n] = emb[:HALF]
        held[1, n] = emb[HALF:]
        turned[n] = emb.T

    def relayed(hop):
        return pltpu.make_async_remote_copy(
            src_ref=send.at[0, pl.ds(0, 2)] if hop == 0 else via,
            dst_ref=via if hop == 0 else negs.at[STEPS - 1],
            send_sem=s3.at[STEPS - 1 + hop],
            recv_sem=r3.at[STEPS - 1 + hop],
            device_id=to(1, 3),
            device_id_type=MESH,
        )

    def give(n):
        s = STEPS - 1 - n
        return pltpu.make_async_remote_copy(
            src_ref=send.at[0, pl.ds(2 * n, 2)],
            dst_ref=negs.at[s],
            send_sem=s3.at[s],
            recv_sem=r3.at[s],
            device_id=lane_id(s + 1),
            device_id_type=MESH,
        )

    def one_block(n, c):
        attend(n, c)
        turn_of = tab[TURN + sched[STEPS - 1 - n, lane]]
        send[0, 2 * n] = held[0, turn_of]
        send[0, 2 * n + 1] = held[1, turn_of]

        @pl.when(n == 0)
        def _():
            relayed(0).start()

        @pl.when(n > 0)
        def _():
            give(n).start()

        @pl.when(n == 4)
        def _():
            relayed(0).wait_recv()
            relayed(1).start()

        return c

    lax.fori_loop(0, NB, one_block, 0)

    for b in range(NB):
        for rt in range(2):
            send[1, 2 * b + rt] = held[rt, tab[TURN + b]]
    done = [
        pltpu.make_async_copy(
            send.at[1, pl.ds(2 * b + rt, 1)],
            out.at[pl.ds(b, 1), pl.ds(rt * HALF, HALF), :],
            esem.at[2 * b + rt],
        )
        for b in range(NB)
        for rt in range(2)
    ]
    for c in done:
        c.start()
    for c in load_pos:
        c.wait()

    scale = 1.0 / math.sqrt(D)
    for b in range(NB):
        turn_of = tab[TURN + b]
        fold = jnp.zeros((TILE, TILE), F32)
        own = jnp.concatenate([held[0, turn_of], held[1, turn_of]], axis=0).astype(F32)
        near_by = jnp.concatenate([far[0, b], far[1, b]], axis=0).astype(F32)
        prod = own * near_by
        for k in range(D // TILE):
            fold = fold + prod[:, k * TILE : (k + 1) * TILE]
        row = jnp.sum(fold.T, axis=0, keepdims=True) * scale
        positive[b] = jnp.broadcast_to(row, (8, TILE))

    own_type = [tab[OTYPE + tab[BLOCK + n]] for n in range(NB)]
    base = [
        jnp.concatenate(
            [positive[tab[BLOCK + n]][0:1], positive[tab[BLOCK + n + 1]][0:1]],
            axis=1,
        )
        for n in range(0, NB, 2)
    ]

    def against(s, state):
        frm = (lane + LANES - s - 1) % LANES
        kind = types[frm * NB + sched[s, frm]]
        both = jnp.concatenate([negs[s, 0], negs[s, 1]], axis=0)
        new = []
        for m in range(NB // 2):
            high, den = state[2 * m], state[2 * m + 1]
            emb = jnp.concatenate([turned[2 * m], turned[2 * m + 1]], axis=1)
            even = jnp.where(own_type[2 * m] == kind, 0.0, -jnp.inf)
            odd = jnp.where(own_type[2 * m + 1] == kind, 0.0, -jnp.inf)
            v = dot(both, emb) * scale + jnp.where(left, even, odd)
            top = jnp.maximum(high, jnp.max(v, axis=0, keepdims=True))
            den = den * jnp.exp(high - top) + jnp.sum(jnp.exp(v - top), axis=0, keepdims=True)
            new += [top, den]
        return tuple(new)

    state = []
    for m in range(NB // 2):
        state += [base[m], jnp.ones((1, WIN), F32)]
    for s in reversed(range(STEPS - 1)):
        give(STEPS - 1 - s).wait_recv()
        state = against(s, state)
    relayed(1).wait_recv()
    state = against(STEPS - 1, state)

    total = jnp.zeros((1, TILE), F32)
    for m in range(NB // 2):
        row = state[2 * m] + jnp.log(state[2 * m + 1]) - base[m]
        for i in range(2):
            n = 2 * m + i
            one = row[:, i * TILE : (i + 1) * TILE]
            total = total + one * weight[own_type[n]]
            rows_of[n] = jnp.broadcast_to(one, (8, TILE))
    subtotal[...] = jnp.broadcast_to(total, (8, TILE))

    def lane_copy(by):
        return pltpu.make_async_remote_copy(
            src_ref=subtotal,
            dst_ref=lanes.at[by],
            send_sem=sl.at[by],
            recv_sem=rl.at[by],
            device_id=lane_id(by),
            device_id_type=MESH,
        )

    for by in range(1, LANES):
        lane_copy(by).start()
    for b in range(NB):
        loss[b : b + 1, :] = rows_of[tab[TURN + b]][0:1]
    lanes[0] = subtotal[...]
    for by in range(1, LANES):
        lane_copy(by).wait_recv()
    acc = lanes[lane]
    for k in range(1, LANES):
        acc = acc + lanes[(lane + LANES - k) % LANES]
    doms[0] = acc

    def dom_copy(by):
        return pltpu.make_async_remote_copy(
            src_ref=doms.at[0],
            dst_ref=doms.at[by],
            send_sem=sd.at[by],
            recv_sem=rd.at[by],
            device_id=dom_id(by),
            device_id_type=MESH,
        )

    for by in range(1, 8):
        dom_copy(by).start()
    for c in done:
        c.wait()
    relayed(0).wait_send()
    relayed(1).wait_send()
    for n in range(1, STEPS):
        give(n).wait_send()
    for by in range(1, LANES):
        lane_copy(by).wait_send()
    for by in range(1, 8):
        dom_copy(by).wait_recv()
    acc = doms[dom]
    for k in range(1, 8):
        acc = acc + doms[(dom + 8 - k) % 8]
    whole = jnp.sum(acc, axis=1, keepdims=True) * (1.0 / (NB * TILE * 128))
    mean[...] = jnp.broadcast_to(whole, (8, TILE))
    for by in range(1, 8):
        dom_copy(by).wait_send()


def layer(*operands):
    smem = pl.BlockSpec(memory_space=pltpu.SMEM)
    vmem = pl.BlockSpec(memory_space=pltpu.VMEM)
    hbm = pl.BlockSpec(memory_space=pl.ANY)
    dma = pltpu.SemaphoreType.DMA
    return pl.pallas_call(
        layer_kernel,
        name="layer",
        out_shape=(
            jax.ShapeDtypeStruct((NB, TILE, D), BF),
            jax.ShapeDtypeStruct((NB, TILE), F32),
            jax.ShapeDtypeStruct((8, TILE), F32),
        ),
        in_specs=[smem] * 7 + [hbm] * 8,
        out_specs=(hbm, vmem, vmem),
        scratch_shapes=[
            pltpu.SMEM((TABLE,), jnp.int32),
            *[pltpu.VMEM((2, NB, HALF, D), BF)] * 4,
            pltpu.VMEM((2, 36, HALF, D), BF),
            pltpu.VMEM((2, 36, HALF, D), BF),
            pltpu.VMEM((2, 36, HALF, D), BF),
            pltpu.VMEM((2, 12, HALF, D), BF),
            pltpu.VMEM((3, D, D), BF),
            pltpu.VMEM((3, D, D), BF),
            pltpu.VMEM((3, D, D), BF),
            pltpu.VMEM((NREL, D, DH), BF),
            pltpu.VMEM((NREL, STRIPS, WIN), BF),
            pltpu.VMEM((NREL, STRIPS, WIN), BF),
            pltpu.VMEM((NB, D, TILE), BF),
            pltpu.VMEM((REQ, TILE, D), BF),
            pltpu.VMEM((REQ, D, TILE), BF),
            pltpu.VMEM((HEADS // 2, WIN, WIN), BF),
            pltpu.VMEM((D, TILE), F32),
            pltpu.VMEM((STEPS, 2, HALF, D), BF),
            pltpu.VMEM((2, HALF, D), BF),
            pltpu.VMEM((NB, 8, TILE), F32),
            pltpu.VMEM((NB, 8, TILE), F32),
            pltpu.VMEM((8, TILE), F32),
            pltpu.VMEM((LANES, 8, TILE), F32),
            pltpu.VMEM((8, 8, TILE), F32),
            dma((2,)),
            dma((6,)),
            dma((2 * NB,)),
            dma((2, 2, 3)),
            dma((2, 2, 3)),
            dma((2, 4, 4)),
            dma((2, 4, 4)),
            dma((STEPS + 1,)),
            dma((STEPS + 1,)),
            dma((LANES,)),
            dma((LANES,)),
            dma((8,)),
            dma((8,)),
        ],
        compiler_params=pltpu.CompilerParams(
            collective_id=0, has_side_effects=True, vmem_limit_bytes=67043328
        ),
    )(*operands)


def shards(
    feats,
    node_type,
    tiles,
    relation,
    neg_sched,
    w_query,
    w_key,
    w_value,
    w_out,
    rel_att,
    rel_msg,
    rel_prior,
    skip_gate,
    pos_view,
    type_weight,
):
    blocks = feats.reshape(NB, TILE, D)
    emb, loss, mean = layer(
        tiles.T,
        node_type,
        relation.T,
        neg_sched.T,
        rel_prior,
        skip_gate,
        type_weight,
        blocks,
        pos_view.reshape(NB, TILE, D),
        w_query,
        w_key,
        w_value,
        w_out,
        rel_att.reshape(NREL, D, DH),
        rel_msg.reshape(NREL, D, DH),
    )
    return emb.reshape(NB * TILE, D), loss.reshape(NB * TILE), mean[0, 0]


def solution(mesh):
    finer = Mesh(mesh.devices.reshape(4, 2, 4, 4), DOM_NARROW)
    in_specs = (
        P(DOM_NARROW, None),
        P(DOM),
        P(DOM, None),
        P(DOM_NARROW, None),
        P(DOM, None),
        P(),
        P(),
        P(),
        P(),
        P(),
        P(),
        P(),
        P(),
        P(DOM_NARROW, None),
        P(),
    )
    out_specs = (P(DOM_NARROW, None), P(DOM_NARROW), P())
    return jax.shard_map(
        shards, mesh=finer, in_specs=in_specs, out_specs=out_specs, check_vma=False
    )
```

```python
import functools
import math

import jax
import jax.numpy as jnp
from jax import lax
from jax.experimental import pallas as pl
from jax.experimental.pallas import tpu as pltpu
from jax.sharding import Mesh
from jax.sharding import PartitionSpec as P

D = 768
HEADS = 8
DH = 96
TILE = 128
HALF = TILE // 2
NT = 4
NB = 8
REQ = NB * NT
RING = 4
CAP = 3
NREL = 5
STEPS = 8
LANES = 16
WIN = 256
STRIP = [(0, 384), (128, 640), (384, 768)]
DOM_NARROW = ("dom_0", "dom_1", "narrow_0", "narrow_1")
DOM = ("dom_0", "dom_1")
MESH = pl.DeviceIdType.MESH
BF = jnp.bfloat16
F32 = jnp.float32

SEL = 0
IDX = 72
STYPE = 136
RELA = 168
PLACE = 200
ORDER = 232
STAGE = 264
OTYPE = 296
FIRST = 304
TURN = 312
BLOCK = 320
TABLE = 328
READY = [5, 11, 17, 26, 32]
STAGE_OF = {
    (1, 3): 1, (3, 1): 1, (2, 3): 2, (3, 2): 2, (1, 2): 3, (2, 1): 3, (2, 2): 3, (1, 1): 4, (3, 3): 4,
}
STRIP_AT = [0, 384, 896]
STRIPS = 1280
PAIR = [0, 128, 384, 512]


def dot(a, b):
    return jnp.dot(a, b, preferred_element_type=F32)


def dot_t(a, b):
    return lax.dot_general(a, b, (((1,), (1,)), ((), ())), preferred_element_type=F32)


def head_of(index):
    return sum((index >= DH * h).astype(jnp.int32) for h in range(1, HEADS))


def widen(rel, wide):
    for c, (lo, hi) in enumerate(STRIP):
        col = lax.broadcasted_iota(jnp.int32, (DH, WIN), 1) + c * WIN
        row = lax.broadcasted_iota(jnp.int32, (DH, WIN), 0)
        place = (col - DH * head_of(col) == row).astype(F32).astype(BF)
        full = dot(rel[lo:hi, :], place)
        col = lax.broadcasted_iota(jnp.int32, (hi - lo, WIN), 1) + c * WIN
        row = lax.broadcasted_iota(jnp.int32, (hi - lo, WIN), 0) + lo
        full = jnp.where(head_of(row) == head_of(col), full, 0.0)
        wide[STRIP_AT[c] : STRIP_AT[c] + hi - lo, :] = full.astype(BF)


def spread(rows, wide):
    return jnp.concatenate(
        [
            dot(rows[:, lo:hi], wide[STRIP_AT[c] : STRIP_AT[c] + hi - lo, :])
            for c, (lo, hi) in enumerate(STRIP)
        ],
        axis=1,
    )


def layer_kernel(
    tiles, types, relation, sched, prior, gate, weight, feats, pos, wq, wk, wv, wo, att, msg,
    out, loss, mean,
    tab, near0, near1, near2, near3, far, held, send, transit,
    wqo, wks, wvs, raw, att_wide, msg_wide, turned, keyed, message, pairs, agg,
    negs, via, positive, rows_of, subtotal, lanes, doms,
    lsem, wsem, esem, s1, r1, s2, r2, s3, r3, s4, r4, sl, rl, sd, rd,
):
    z = lax.axis_index("narrow_0")
    x = lax.axis_index("narrow_1")
    lane = z * RING + x
    coord = [x, z]
    name = ["narrow_1", "narrow_0"]
    near = [near0, near1, near2, near3]

    def to(axis, by):
        return {name[axis]: (coord[axis] + by) % RING}

    local = [
        pltpu.make_async_copy(feats.at[:, pl.ds(rt * HALF, HALF), :], near0.at[rt], lsem.at[rt])
        for rt in range(2)
    ]
    for c in local:
        c.start()
    dom = lax.axis_index("dom_0") * 2 + lax.axis_index("dom_1")

    def lane_id(by):
        other = (lane + by) % LANES
        return {"narrow_0": other // RING, "narrow_1": other % RING}

    def dom_id(by):
        other = (dom + by) % 8
        return {"dom_0": other // 2, "dom_1": other % 2}

    barrier = pltpu.get_barrier_semaphore()
    for by in range(1, LANES):
        pl.semaphore_signal(barrier, 1, device_id=lane_id(by), device_id_type=MESH)
    for by in range(1, 8):
        pl.semaphore_signal(barrier, 1, device_id=dom_id(by), device_id_type=MESH)
    pl.semaphore_wait(barrier, LANES - 1 + 7)
    for c in local:
        c.wait()

    def first(rt, way, part):
        by = slot = (1, 3)[way]
        half = part if way == 0 else 1 - part
        return pltpu.make_async_remote_copy(
            src_ref=near0.at[rt, pl.ds(half * 4, 4)],
            dst_ref=near[slot].at[rt, pl.ds(half * 4, 4)],
            send_sem=s1.at[rt, way, part],
            recv_sem=r1.at[rt, way, part],
            device_id=to(rt, by),
            device_id_type=MESH,
        )

    def forward(rt, way):
        by = slot = (1, 3)[way]
        return pltpu.make_async_remote_copy(
            src_ref=near[slot].at[rt, pl.ds(way * 4, 4)],
            dst_ref=near2.at[rt, pl.ds(way * 4, 4)],
            send_sem=s1.at[rt, way, 2],
            recv_sem=r1.at[rt, way, 2],
            device_id=to(rt, by),
            device_id_type=MESH,
        )

    def second(rt, d, o):
        at = pl.ds((d - 1) * 12 + o * CAP, CAP)
        if d == 2:
            dst = transit.at[rt, pl.ds(o * CAP, CAP)]
            by = 1 if o < 2 else 3
        else:
            dst = far.at[rt, at]
            by = d
        return pltpu.make_async_remote_copy(
            src_ref=send.at[rt, at],
            dst_ref=dst,
            send_sem=s2.at[rt, d - 1, o],
            recv_sem=r2.at[rt, d - 1, o],
            device_id=to(1 - rt, by),
            device_id_type=MESH,
        )

    def onward(rt, o):
        return pltpu.make_async_remote_copy(
            src_ref=transit.at[rt, pl.ds(o * CAP, CAP)],
            dst_ref=far.at[rt, pl.ds(12 + o * CAP, CAP)],
            send_sem=s2.at[rt, 3, o],
            recv_sem=r2.at[rt, 3, o],
            device_id=to(1 - rt, 1 if o < 2 else 3),
            device_id_type=MESH,
        )

    def pick(o, last=0):
        for d in (2, 1, 3):
            for rt in range(2):
                for k in range(CAP):
                    at = (d - 1) * 12 + o * CAP + k
                    send[rt, at] = near[o][rt, tab[SEL + rt * 36 + at]]
                if d != last:
                    second(rt, d, o).start()

    def take(d, o):
        at = (d - 1) * 12 + o * CAP
        for rt in range(2):
            (onward(rt, o) if d == 2 else second(rt, d, o)).wait_recv()
            held[rt, at : at + CAP] = far[rt, at : at + CAP]

    def relay(o):
        for rt in range(2):
            second(rt, 2, o).wait_recv()
            onward(rt, o).start()

    for part in range(2):
        for rt in range(2):
            for way in range(2):
                first(rt, way, part).start()
    load_wq = pltpu.make_async_copy(wq, wqo, wsem.at[0])
    load_wk = pltpu.make_async_copy(wk, wks, wsem.at[1])
    load_wv = pltpu.make_async_copy(wv, wvs, wsem.at[2])
    load_att = pltpu.make_async_copy(att, raw, wsem.at[3])
    load_msg = pltpu.make_async_copy(msg, raw, wsem.at[4])
    load_wo = pltpu.make_async_copy(wo, wqo, wsem.at[5])
    load_att.start()
    load_wq.start()
    load_wk.start()
    load_wv.start()

    for rt in range(2):
        for d in range(1, RING):
            if rt == 0:
                dst = (z + d) % RING * RING + x
            else:
                dst = z * RING + (x + d) % RING

            def ask(p, c, rt=rt, dst=dst):
                c = list(c)
                t = tiles[p % NT, dst * NB + p // NT]
                owner = t // NB
                oz = (z - owner // RING + RING) % RING
                ox = (x - owner % RING + RING) % RING
                here, o = (oz, ox) if rt == 0 else (ox, oz)
                for i in range(RING):
                    hit = jnp.logical_and(here == 0, o == i)
                    c[i] = jnp.where(hit, c[i] + c[RING + i] * (t % NB), c[i])
                    c[RING + i] = jnp.where(hit, c[RING + i] * NB, c[RING + i])
                return tuple(c)

            got = lax.fori_loop(
                0, REQ, ask, (jnp.int32(0),) * RING + (jnp.int32(1),) * RING
            )
            for o in range(RING):
                for k in range(CAP):
                    tab[SEL + rt * 36 + (d - 1) * 12 + o * CAP + k] = (
                        got[o] // NB**k
                    ) % NB
    pick(0)

    def mine(p, c):
        c = list(c)
        t = tiles[p % NT, lane * NB + p // NT]
        owner = t // NB
        oz = (z - owner // RING + RING) % RING
        ox = (x - owner % RING + RING) % RING
        back = oz * RING + ox
        k = jnp.int32(0)
        for i in range(LANES):
            hit = back == i
            k = jnp.where(hit, c[i], k)
            c[i] = jnp.where(hit, c[i] + 1, c[i])
        stage = jnp.int32(0)
        for (a, b), v in STAGE_OF.items():
            stage = jnp.where(back == a * RING + b, v, stage)
        tab[IDX + p] = jnp.where(
            oz == 0, ox * NB + t % NB, 32 + (oz - 1) * 12 + ox * CAP + k
        )
        tab[IDX + REQ + p] = jnp.where(
            ox == 0, oz * NB + t % NB, 32 + (ox - 1) * 12 + oz * CAP + k
        )
        tab[STYPE + p] = types[t]
        tab[RELA + p] = relation[p % NT, p // NT]
        tab[STAGE + p] = stage
        for v in range(4):
            c[LANES + v] = c[LANES + v] + jnp.where(stage <= v, 1, 0)
        return tuple(c)

    counts = lax.fori_loop(0, REQ, mine, (jnp.int32(0),) * (LANES + 4))[LANES:]

    def turn(p, c):
        c = list(c)
        stage = tab[STAGE + p]
        place = jnp.int32(0)
        for v in range(5):
            hit = stage == v
            place = jnp.where(hit, c[v], place)
            c[v] = jnp.where(hit, c[v] + 1, c[v])
        tab[PLACE + p] = place
        return tuple(c)

    lax.fori_loop(0, REQ, turn, (jnp.int32(0),) + tuple(counts))

    def invert(n, c):
        found = jnp.int32(0)
        for p in range(REQ):
            found = jnp.where(tab[PLACE + p] == n, p, found)
        tab[ORDER + n] = found
        return c

    lax.fori_loop(0, REQ, invert, 0)
    for b in range(NB):
        tab[OTYPE + b] = types[lane * NB + b]
        at = jnp.int32(STEPS + b)
        for n in reversed(range(STEPS)):
            at = jnp.where(sched[STEPS - 1 - n, lane] == b, n, at)
        tab[FIRST + b] = at
    for b in range(NB):
        ahead = jnp.int32(0)
        for e in range(NB):
            ahead = ahead + jnp.where(tab[FIRST + e] < tab[FIRST + b], 1, 0)
        tab[TURN + b] = ahead
    for n in range(NB):
        found = jnp.int32(0)
        for b in range(NB):
            found = jnp.where(tab[TURN + b] == n, b, found)
        tab[BLOCK + n] = found
    pairs[...] = jnp.zeros_like(pairs)

    def widen_all(wide):
        def body(r, c):
            widen(raw.at[r], wide.at[r])
            return c

        lax.fori_loop(0, NREL, body, 0)

    load_att.wait()
    widen_all(att_wide)
    load_msg.start()
    for rt in range(2):
        for way in range(2):
            first(rt, way, 0).wait_recv()
            forward(rt, way).start()

    load_wq.wait()

    def ask_query(n, c):
        b = tab[BLOCK + n]
        rows = jnp.concatenate([near0[0, b], near0[1, b]], axis=0)
        turned[n] = dot(rows, wqo[tab[OTYPE + b]]).astype(BF).T
        return c

    lax.fori_loop(0, NB, ask_query, 0)
    load_wo.start()
    load_msg.wait()
    widen_all(msg_wide)
    load_wk.wait()
    load_wv.wait()
    relay(0)
    for rt in range(2):
        for way in range(2):
            first(rt, way, 1).wait_recv()
    pick(1, last=1)
    pick(3, last=3)
    for rt in range(2):
        for way in range(2):
            forward(rt, way).wait_recv()
    pick(2)

    def part_of(rt, i):
        rows = held[rt, jnp.clip(i - 32, 0, 35)]
        for o in range(RING):
            rows = jnp.where(i // NB == o, near[o][rt, jnp.clip(i - o * NB, 0, NB - 1)], rows)
        return rows

    def transform(n, c):
        p = tab[ORDER + n]
        src = jnp.concatenate(
            [part_of(0, tab[IDX + p]), part_of(1, tab[IDX + REQ + p])], axis=0
        )
        ts = tab[STYPE + p]
        r = tab[RELA + p]
        key = dot(src, wks[ts]).astype(BF)
        keyed[n] = spread(key, att_wide.at[r]).astype(BF)
        value = dot(src, wvs[ts]).astype(BF)
        message[n] = spread(value, msg_wide.at[r]).astype(BF).T
        return c

    take(3, 0)
    take(1, 0)
    take(2, 0)
    relay(3)
    lax.fori_loop(0, READY[0], transform, 0)
    relay(1)
    for rt in range(2):
        second(rt, 1, 1).start()
    relay(2)
    for rt in range(2):
        second(rt, 3, 3).start()
    take(3, 1)
    take(1, 3)
    lax.fori_loop(READY[0], READY[1], transform, 0)
    take(3, 2)
    take(2, 3)
    lax.fori_loop(READY[1], READY[2], transform, 0)
    take(1, 2)
    take(2, 1)
    take(2, 2)
    lax.fori_loop(READY[2], READY[3], transform, 0)
    take(1, 1)
    take(3, 3)
    lax.fori_loop(READY[3], READY[4], transform, 0)

    for rt in range(2):
        for way in range(2):
            for part in range(2):
                first(rt, way, part).wait_send()
            forward(rt, way).wait_send()
        for o in range(4):
            for d in (1, 2, 3):
                second(rt, d, o).wait_send()
            onward(rt, o).wait_send()
    load_wo.wait()

    load_pos = [
        pltpu.make_async_copy(
            pos.at[:, pl.ds(rt * HALF, HALF), :], far.at[rt, pl.ds(0, NB)], lsem.at[rt]
        )
        for rt in range(2)
    ]
    for c in load_pos:
        c.start()

    left = lax.broadcasted_iota(jnp.int32, (1, WIN), 1) < TILE
    unit = math.log2(math.e) / math.sqrt(DH)

    def attend(n, c):
        b = tab[BLOCK + n]
        where = [tab[PLACE + b * NT + j] for j in range(NT)]
        rel = [tab[RELA + b * NT + j] for j in range(NT)]
        for h in range(HEADS):
            lo = h * DH - PAIR[h // 2]
            pairs[h // 2, lo : lo + DH, h % 2 * TILE : (h % 2 + 1) * TILE] = turned[
                n, h * DH : (h + 1) * DH, :
            ]
        for q in range(HEADS // 2):
            w = PAIR[q]
            scores = []
            for j in range(NT):
                scale = jnp.where(left, prior[rel[j], 2 * q], prior[rel[j], 2 * q + 1]) * unit
                scores.append(dot(keyed[where[j], :, w : w + WIN], pairs[q]) * scale)
            top = jnp.maximum(
                jnp.maximum(scores[0], scores[1]), jnp.maximum(scores[2], scores[3])
            )
            top = jnp.max(top, axis=0, keepdims=True)
            weights = [jnp.exp2(s - top) for s in scores]
            total = jnp.sum(
                (weights[0] + weights[1]) + (weights[2] + weights[3]), axis=0, keepdims=True
            )
            inv = 1.0 / total
            rows = slice(2 * q * DH, (2 * q + 2) * DH)
            lhs = jnp.concatenate([message[where[j], rows, :] for j in range(NT)], axis=1)
            got = dot(lhs, jnp.concatenate([e.astype(BF) for e in weights], axis=0))
            agg[2 * q * DH : (2 * q + 1) * DH, :] = got[:DH, :TILE] * inv[:, :TILE]
            agg[(2 * q + 1) * DH : (2 * q + 2) * DH, :] = got[DH:, TILE:] * inv[:, TILE:]
        merged = agg[...]
        active = (0.5 * merged * (1.0 + lax.erf(merged * math.sqrt(0.5)))).astype(BF).T
        tb = tab[OTYPE + b]
        projected = dot(active, wqo[tb])
        a = jax.nn.sigmoid(jnp.full((1, D), gate[tb], F32))
        own = jnp.concatenate([near0[0, b], near0[1, b]], axis=0).astype(F32)
        emb = (a * projected + (1.0 - a) * own).astype(BF)
        held[0, n] = emb[:HALF]
        held[1, n] = emb[HALF:]
        turned[n] = emb.T

    def give(n):
        s = STEPS - 1 - n
        return pltpu.make_async_remote_copy(
            src_ref=send.at[0, pl.ds(2 * n, 2)],
            dst_ref=negs.at[s],
            send_sem=s3.at[s],
            recv_sem=r3.at[s],
            device_id=lane_id(s + 1),
            device_id_type=MESH,
        )

    def to_via(n):
        return pltpu.make_async_remote_copy(
            src_ref=send.at[0, pl.ds(2 * n, 2)],
            dst_ref=via.at[n],
            send_sem=s3.at[STEPS - 1 - n],
            recv_sem=r4.at[n],
            device_id={"narrow_0": (z + 3) % RING, "narrow_1": (x + RING - n) % RING},
            device_id_type=MESH,
        )

    def from_via(n):
        return pltpu.make_async_remote_copy(
            src_ref=via.at[n],
            dst_ref=negs.at[STEPS - 1 - n],
            send_sem=s4.at[n],
            recv_sem=r3.at[STEPS - 1 - n],
            device_id=to(1, 3),
            device_id_type=MESH,
        )

    def one_block(n, c):
        attend(n, c)
        turn_of = tab[TURN + sched[STEPS - 1 - n, lane]]
        send[0, 2 * n] = held[0, turn_of]
        send[0, 2 * n + 1] = held[1, turn_of]

        @pl.when(n == 0)
        def _():
            to_via(0).start()

        @pl.when(jnp.logical_and(n == 1, x > 0))
        def _():
            to_via(1).start()

        @pl.when(jnp.logical_and(n == 1, x == 0))
        def _():
            give(1).start()

        @pl.when(n > 1)
        def _():
            give(n).start()

        @pl.when(n == 3)
        def _():
            to_via(0).wait_recv()
            from_via(0).start()

        @pl.when(jnp.logical_and(n == 5, x < RING - 1))
        def _():
            to_via(1).wait_recv()
            from_via(1).start()

        return c

    lax.fori_loop(0, NB, one_block, 0)

    for b in range(NB):
        for rt in range(2):
            send[1, 2 * b + rt] = held[rt, tab[TURN + b]]
    done = [
        pltpu.make_async_copy(
            send.at[1, pl.ds(2 * b + rt, 1)],
            out.at[pl.ds(b, 1), pl.ds(rt * HALF, HALF), :],
            esem.at[2 * b + rt],
        )
        for b in range(NB)
        for rt in range(2)
    ]
    for c in done:
        c.start()
    for c in load_pos:
        c.wait()

    scale = 1.0 / math.sqrt(D)
    for b in range(NB):
        turn_of = tab[TURN + b]
        fold = jnp.zeros((TILE, TILE), F32)
        own = jnp.concatenate([held[0, turn_of], held[1, turn_of]], axis=0).astype(F32)
        near_by = jnp.concatenate([far[0, b], far[1, b]], axis=0).astype(F32)
        prod = own * near_by
        for k in range(D // TILE):
            fold = fold + prod[:, k * TILE : (k + 1) * TILE]
        row = jnp.sum(fold.T, axis=0, keepdims=True) * scale
        positive[b] = jnp.broadcast_to(row, (8, TILE))

    own_type = [tab[OTYPE + tab[BLOCK + n]] for n in range(NB)]
    base = [
        jnp.concatenate(
            [positive[tab[BLOCK + n]][0:1], positive[tab[BLOCK + n + 1]][0:1]],
            axis=1,
        )
        for n in range(0, NB, 2)
    ]

    def against(s, state):
        frm = (lane + LANES - s - 1) % LANES
        kind = types[frm * NB + sched[s, frm]]
        both = jnp.concatenate([negs[s, 0], negs[s, 1]], axis=0)
        new = []
        for m in range(NB // 2):
            high, den = state[2 * m], state[2 * m + 1]
            emb = jnp.concatenate([turned[2 * m], turned[2 * m + 1]], axis=1)
            even = jnp.where(own_type[2 * m] == kind, 0.0, -jnp.inf)
            odd = jnp.where(own_type[2 * m + 1] == kind, 0.0, -jnp.inf)
            v = dot(both, emb) * scale + jnp.where(left, even, odd)
            top = jnp.maximum(high, jnp.max(v, axis=0, keepdims=True))
            den = den * jnp.exp(high - top) + jnp.sum(jnp.exp(v - top), axis=0, keepdims=True)
            new += [top, den]
        return tuple(new)

    state = []
    for m in range(NB // 2):
        state += [base[m], jnp.ones((1, WIN), F32)]
    for s in (5, 4, 7, 3, 6, 2, 1, 0):
        give(STEPS - 1 - s).wait_recv()
        state = against(s, state)

    total = jnp.zeros((1, TILE), F32)
    for m in range(NB // 2):
        row = state[2 * m] + jnp.log(state[2 * m + 1]) - base[m]
        for i in range(2):
            n = 2 * m + i
            one = row[:, i * TILE : (i + 1) * TILE]
            total = total + one * weight[own_type[n]]
            rows_of[n] = jnp.broadcast_to(one, (8, TILE))
    subtotal[...] = jnp.broadcast_to(total, (8, TILE))

    def lane_copy(by):
        return pltpu.make_async_remote_copy(
            src_ref=subtotal,
            dst_ref=lanes.at[by],
            send_sem=sl.at[by],
            recv_sem=rl.at[by],
            device_id=lane_id(by),
            device_id_type=MESH,
        )

    for by in range(1, LANES):
        lane_copy(by).start()
    for b in range(NB):
        loss[b : b + 1, :] = rows_of[tab[TURN + b]][0:1]
    lanes[0] = subtotal[...]
    for by in range(1, LANES):
        lane_copy(by).wait_recv()
    acc = lanes[lane]
    for k in range(1, LANES):
        acc = acc + lanes[(lane + LANES - k) % LANES]
    doms[0] = acc

    def dom_copy(by):
        return pltpu.make_async_remote_copy(
            src_ref=doms.at[0],
            dst_ref=doms.at[by],
            send_sem=sd.at[by],
            recv_sem=rd.at[by],
            device_id=dom_id(by),
            device_id_type=MESH,
        )

    for by in range(1, 8):
        dom_copy(by).start()
    for c in done:
        c.wait()
    for n in range(STEPS):
        give(n).wait_send()
    from_via(0).wait_send()

    @pl.when(x < RING - 1)
    def _():
        from_via(1).wait_send()

    for by in range(1, LANES):
        lane_copy(by).wait_send()
    for by in range(1, 8):
        dom_copy(by).wait_recv()
    acc = doms[dom]
    for k in range(1, 8):
        acc = acc + doms[(dom + 8 - k) % 8]
    whole = jnp.sum(acc, axis=1, keepdims=True) * (1.0 / (NB * TILE * 128))
    mean[...] = jnp.broadcast_to(whole, (8, TILE))
    for by in range(1, 8):
        dom_copy(by).wait_send()


def layer(*operands):
    smem = pl.BlockSpec(memory_space=pltpu.SMEM)
    vmem = pl.BlockSpec(memory_space=pltpu.VMEM)
    hbm = pl.BlockSpec(memory_space=pl.ANY)
    dma = pltpu.SemaphoreType.DMA
    return pl.pallas_call(
        layer_kernel,
        name="layer",
        out_shape=(
            jax.ShapeDtypeStruct((NB, TILE, D), BF),
            jax.ShapeDtypeStruct((NB, TILE), F32),
            jax.ShapeDtypeStruct((8, TILE), F32),
        ),
        in_specs=[smem] * 7 + [hbm] * 8,
        out_specs=(hbm, vmem, vmem),
        scratch_shapes=[
            pltpu.SMEM((TABLE,), jnp.int32),
            *[pltpu.VMEM((2, NB, HALF, D), BF)] * 4,
            pltpu.VMEM((2, 36, HALF, D), BF),
            pltpu.VMEM((2, 36, HALF, D), BF),
            pltpu.VMEM((2, 36, HALF, D), BF),
            pltpu.VMEM((2, 12, HALF, D), BF),
            pltpu.VMEM((3, D, D), BF),
            pltpu.VMEM((3, D, D), BF),
            pltpu.VMEM((3, D, D), BF),
            pltpu.VMEM((NREL, D, DH), BF),
            pltpu.VMEM((NREL, STRIPS, WIN), BF),
            pltpu.VMEM((NREL, STRIPS, WIN), BF),
            pltpu.VMEM((NB, D, TILE), BF),
            pltpu.VMEM((REQ, TILE, D), BF),
            pltpu.VMEM((REQ, D, TILE), BF),
            pltpu.VMEM((HEADS // 2, WIN, WIN), BF),
            pltpu.VMEM((D, TILE), F32),
            pltpu.VMEM((STEPS, 2, HALF, D), BF),
            pltpu.VMEM((2, 2, HALF, D), BF),
            pltpu.VMEM((NB, 8, TILE), F32),
            pltpu.VMEM((NB, 8, TILE), F32),
            pltpu.VMEM((8, TILE), F32),
            pltpu.VMEM((LANES, 8, TILE), F32),
            pltpu.VMEM((8, 8, TILE), F32),
            dma((2,)),
            dma((6,)),
            dma((2 * NB,)),
            dma((2, 2, 3)),
            dma((2, 2, 3)),
            dma((2, 4, 4)),
            dma((2, 4, 4)),
            dma((STEPS,)),
            dma((STEPS,)),
            dma((2,)),
            dma((2,)),
            dma((LANES,)),
            dma((LANES,)),
            dma((8,)),
            dma((8,)),
        ],
        compiler_params=pltpu.CompilerParams(
            collective_id=0, has_side_effects=True, vmem_limit_bytes=67043328
        ),
    )(*operands)


def finish_kernel(emb, loss, mean, emb_out, loss_out, mean_out, buf, came, went):
    def come(i):
        return pltpu.make_async_copy(emb.at[i], buf.at[i], came.at[i])

    def go(i):
        return pltpu.make_async_copy(buf.at[i], emb_out.at[i], went.at[i])

    for i in range(NB):
        come(i).start()
    loss_out[...] = loss[...]
    mean_out[...] = mean[0:1, 0:1]
    for i in range(NB):
        come(i).wait()
        go(i).start()
    for i in range(NB):
        go(i).wait()


def finish(emb, loss, mean):
    vmem = pl.BlockSpec(memory_space=pltpu.VMEM)
    hbm = pl.BlockSpec(memory_space=pl.ANY)
    return pl.pallas_call(
        finish_kernel,
        name="finish",
        out_shape=(
            jax.ShapeDtypeStruct((NB, TILE, D), BF),
            jax.ShapeDtypeStruct((NB, TILE), F32),
            jax.ShapeDtypeStruct((1, 1), F32),
        ),
        in_specs=[hbm, vmem, vmem],
        out_specs=(hbm, vmem, vmem),
        scratch_shapes=[
            pltpu.VMEM((NB, TILE, D), BF),
            pltpu.SemaphoreType.DMA((NB,)),
            pltpu.SemaphoreType.DMA((NB,)),
        ],
    )(emb, loss, mean)


def shards(
    feats,
    node_type,
    tiles,
    relation,
    neg_sched,
    w_query,
    w_key,
    w_value,
    w_out,
    rel_att,
    rel_msg,
    rel_prior,
    skip_gate,
    pos_view,
    type_weight,
):
    blocks = feats.reshape(NB, TILE, D)
    emb, loss, mean = layer(
        tiles.T,
        node_type,
        relation.T,
        neg_sched.T,
        rel_prior,
        skip_gate,
        type_weight,
        blocks,
        pos_view.reshape(NB, TILE, D),
        w_query,
        w_key,
        w_value,
        w_out,
        rel_att.reshape(NREL, D, DH),
        rel_msg.reshape(NREL, D, DH),
    )
    emb, loss, mean = finish(emb, loss, mean)
    return emb.reshape(NB * TILE, D), loss.reshape(NB * TILE), mean[0, 0]


def solution(mesh):
    finer = Mesh(mesh.devices.reshape(4, 2, 4, 4), DOM_NARROW)
    in_specs = (
        P(DOM_NARROW, None),
        P(DOM),
        P(DOM, None),
        P(DOM_NARROW, None),
        P(DOM, None),
        P(),
        P(),
        P(),
        P(),
        P(),
        P(),
        P(),
        P(),
        P(DOM_NARROW, None),
        P(),
    )
    out_specs = (P(DOM_NARROW, None), P(DOM_NARROW), P())
    return jax.shard_map(
        shards, mesh=finer, in_specs=in_specs, out_specs=out_specs, check_vma=False
    )
```

```python
import functools
import math

import jax
import jax.numpy as jnp
from jax import lax
from jax.experimental import pallas as pl
from jax.experimental.pallas import tpu as pltpu
from jax.sharding import Mesh
from jax.sharding import PartitionSpec as P

D = 768
HEADS = 8
DH = 96
TILE = 128
HALF = TILE // 2
NT = 4
NB = 8
REQ = NB * NT
RING = 4
CAP = 3
NREL = 5
STEPS = 8
LANES = 16
WIN = 256
STRIP = [(0, 384), (128, 640), (384, 768)]
DOM_NARROW = ("dom_0", "dom_1", "narrow_0", "narrow_1")
DOM = ("dom_0", "dom_1")
MESH = pl.DeviceIdType.MESH
BF = jnp.bfloat16
F32 = jnp.float32

SEL = 0
IDX = 72
STYPE = 136
RELA = 168
PLACE = 200
ORDER = 232
STAGE = 264
OTYPE = 296
FIRST = 304
TURN = 312
BLOCK = 320
OFFER = 328
TABLE = 336
SENT = (4, 8, 5, 7, 6, 3, 2, 1)
READY = [4, 10, 16, 26, 32]
STAGE_OF = {
    (1, 3): 1, (3, 1): 1, (2, 3): 2, (3, 2): 2, (1, 2): 3, (2, 1): 3, (2, 2): 3, (1, 1): 4, (3, 3): 4,
}
STRIP_AT = [0, 384, 896]
STRIPS = 1280
PAIR = [0, 128, 384, 512]


def dot(a, b):
    return jnp.dot(a, b, preferred_element_type=F32)


def dot_t(a, b):
    return lax.dot_general(a, b, (((1,), (1,)), ((), ())), preferred_element_type=F32)


def head_of(index):
    return sum((index >= DH * h).astype(jnp.int32) for h in range(1, HEADS))


def widen(rel, wide):
    for c, (lo, hi) in enumerate(STRIP):
        col = lax.broadcasted_iota(jnp.int32, (DH, WIN), 1) + c * WIN
        row = lax.broadcasted_iota(jnp.int32, (DH, WIN), 0)
        place = (col - DH * head_of(col) == row).astype(F32).astype(BF)
        full = dot(rel[lo:hi, :], place)
        col = lax.broadcasted_iota(jnp.int32, (hi - lo, WIN), 1) + c * WIN
        row = lax.broadcasted_iota(jnp.int32, (hi - lo, WIN), 0) + lo
        full = jnp.where(head_of(row) == head_of(col), full, 0.0)
        wide[STRIP_AT[c] : STRIP_AT[c] + hi - lo, :] = full.astype(BF)


def spread(rows, wide):
    return jnp.concatenate(
        [
            dot(rows[:, lo:hi], wide[STRIP_AT[c] : STRIP_AT[c] + hi - lo, :])
            for c, (lo, hi) in enumerate(STRIP)
        ],
        axis=1,
    )


def layer_kernel(
    tiles, types, relation, sched, prior, gate, weight, feats, pos, wq, wk, wv, wo, att, msg,
    out, loss, mean,
    tab, near0, near1, near2, near3, far, held, send, transit,
    wqo, wks, wvs, raw, att_wide, msg_wide, turned, keyed, message, pairs, agg,
    negs, via, positive, rows_of, subtotal, lanes, doms,
    lsem, wsem, esem, s1, r1, s2, r2, s3, r3, s4, r4, sl, rl, sd, rd,
):
    z = lax.axis_index("narrow_0")
    x = lax.axis_index("narrow_1")
    lane = z * RING + x
    coord = [x, z]
    name = ["narrow_1", "narrow_0"]
    near = [near0, near1, near2, near3]

    def to(axis, by):
        return {name[axis]: (coord[axis] + by) % RING}

    local = [
        pltpu.make_async_copy(feats.at[:, pl.ds(rt * HALF, HALF), :], near0.at[rt], lsem.at[rt])
        for rt in range(2)
    ]
    for c in local:
        c.start()
    dom = lax.axis_index("dom_0") * 2 + lax.axis_index("dom_1")

    def lane_id(by):
        other = (lane + by) % LANES
        return {"narrow_0": other // RING, "narrow_1": other % RING}

    def dom_id(by):
        other = (dom + by) % 8
        return {"dom_0": other // 2, "dom_1": other % 2}

    barrier = pltpu.get_barrier_semaphore()
    for by in range(1, LANES):
        pl.semaphore_signal(barrier, 1, device_id=lane_id(by), device_id_type=MESH)
    for by in range(1, 8):
        pl.semaphore_signal(barrier, 1, device_id=dom_id(by), device_id_type=MESH)
    pl.semaphore_wait(barrier, LANES - 1 + 7)
    for c in local:
        c.wait()

    def first(rt, way, part):
        by = slot = (1, 3)[way]
        half = part if way == 0 else 1 - part
        return pltpu.make_async_remote_copy(
            src_ref=near0.at[rt, pl.ds(half * 4, 4)],
            dst_ref=near[slot].at[rt, pl.ds(half * 4, 4)],
            send_sem=s1.at[rt, way, part],
            recv_sem=r1.at[rt, way, part],
            device_id=to(rt, by),
            device_id_type=MESH,
        )

    def forward(rt, way):
        by = slot = (1, 3)[way]
        return pltpu.make_async_remote_copy(
            src_ref=near[slot].at[rt, pl.ds(way * 4, 4)],
            dst_ref=near2.at[rt, pl.ds(way * 4, 4)],
            send_sem=s1.at[rt, way, 2],
            recv_sem=r1.at[rt, way, 2],
            device_id=to(rt, by),
            device_id_type=MESH,
        )

    def second(rt, d, o):
        at = pl.ds((d - 1) * 12 + o * CAP, CAP)
        if d == 2:
            dst = transit.at[rt, pl.ds(o * CAP, CAP)]
            by = 1 if o < 2 else 3
        else:
            dst = far.at[rt, at]
            by = d
        return pltpu.make_async_remote_copy(
            src_ref=send.at[rt, at],
            dst_ref=dst,
            send_sem=s2.at[rt, d - 1, o],
            recv_sem=r2.at[rt, d - 1, o],
            device_id=to(1 - rt, by),
            device_id_type=MESH,
        )

    def onward(rt, o):
        return pltpu.make_async_remote_copy(
            src_ref=transit.at[rt, pl.ds(o * CAP, CAP)],
            dst_ref=far.at[rt, pl.ds(12 + o * CAP, CAP)],
            send_sem=s2.at[rt, 3, o],
            recv_sem=r2.at[rt, 3, o],
            device_id=to(1 - rt, 1 if o < 2 else 3),
            device_id_type=MESH,
        )

    def pick(o, last=0):
        for d in (2, 1, 3):
            for rt in range(2):
                for k in range(CAP):
                    at = (d - 1) * 12 + o * CAP + k
                    send[rt, at] = near[o][rt, tab[SEL + rt * 36 + at]]
                if d != last:
                    second(rt, d, o).start()

    def take(d, o):
        at = (d - 1) * 12 + o * CAP
        for rt in range(2):
            (onward(rt, o) if d == 2 else second(rt, d, o)).wait_recv()
            held[rt, at : at + CAP] = far[rt, at : at + CAP]

    def relay(o):
        for rt in range(2):
            second(rt, 2, o).wait_recv()
            onward(rt, o).start()

    for part in range(2):
        for rt in range(2):
            for way in range(2):
                first(rt, way, part).start()
    load_wq = pltpu.make_async_copy(wq, wqo, wsem.at[0])
    load_wk = pltpu.make_async_copy(wk, wks, wsem.at[1])
    load_wv = pltpu.make_async_copy(wv, wvs, wsem.at[2])
    load_att = pltpu.make_async_copy(att, raw, wsem.at[3])
    load_msg = pltpu.make_async_copy(msg, raw, wsem.at[4])
    load_wo = pltpu.make_async_copy(wo, wqo, wsem.at[5])
    load_att.start()
    load_wq.start()
    load_wk.start()
    load_wv.start()

    for rt in range(2):
        for d in range(1, RING):
            if rt == 0:
                dst = (z + d) % RING * RING + x
            else:
                dst = z * RING + (x + d) % RING

            def ask(p, c, rt=rt, dst=dst):
                c = list(c)
                t = tiles[p % NT, dst * NB + p // NT]
                owner = t // NB
                oz = (z - owner // RING + RING) % RING
                ox = (x - owner % RING + RING) % RING
                here, o = (oz, ox) if rt == 0 else (ox, oz)
                for i in range(RING):
                    hit = jnp.logical_and(here == 0, o == i)
                    c[i] = jnp.where(hit, c[i] + c[RING + i] * (t % NB), c[i])
                    c[RING + i] = jnp.where(hit, c[RING + i] * NB, c[RING + i])
                return tuple(c)

            got = lax.fori_loop(
                0, REQ, ask, (jnp.int32(0),) * RING + (jnp.int32(1),) * RING
            )
            for o in range(RING):
                for k in range(CAP):
                    tab[SEL + rt * 36 + (d - 1) * 12 + o * CAP + k] = (
                        got[o] // NB**k
                    ) % NB
    pick(0)

    def mine(p, c):
        c = list(c)
        t = tiles[p % NT, lane * NB + p // NT]
        owner = t // NB
        oz = (z - owner // RING + RING) % RING
        ox = (x - owner % RING + RING) % RING
        back = oz * RING + ox
        k = jnp.int32(0)
        for i in range(LANES):
            hit = back == i
            k = jnp.where(hit, c[i], k)
            c[i] = jnp.where(hit, c[i] + 1, c[i])
        stage = jnp.int32(0)
        for (a, b), v in STAGE_OF.items():
            stage = jnp.where(back == a * RING + b, v, stage)
        tab[IDX + p] = jnp.where(
            oz == 0, ox * NB + t % NB, 32 + (oz - 1) * 12 + ox * CAP + k
        )
        tab[IDX + REQ + p] = jnp.where(
            ox == 0, oz * NB + t % NB, 32 + (ox - 1) * 12 + oz * CAP + k
        )
        tab[STYPE + p] = types[t]
        tab[RELA + p] = relation[p % NT, p // NT]
        tab[STAGE + p] = stage
        for v in range(4):
            c[LANES + v] = c[LANES + v] + jnp.where(stage <= v, 1, 0)
        return tuple(c)

    counts = lax.fori_loop(0, REQ, mine, (jnp.int32(0),) * (LANES + 4))[LANES:]

    def turn(p, c):
        c = list(c)
        stage = tab[STAGE + p]
        place = jnp.int32(0)
        for v in range(5):
            hit = stage == v
            place = jnp.where(hit, c[v], place)
            c[v] = jnp.where(hit, c[v] + 1, c[v])
        tab[PLACE + p] = place
        return tuple(c)

    lax.fori_loop(0, REQ, turn, (jnp.int32(0),) + tuple(counts))

    def invert(n, c):
        found = jnp.int32(0)
        for p in range(REQ):
            found = jnp.where(tab[PLACE + p] == n, p, found)
        tab[ORDER + n] = found
        return c

    lax.fori_loop(0, REQ, invert, 0)
    for b in range(NB):
        tab[OTYPE + b] = types[lane * NB + b]
        at = jnp.int32(STEPS + b)
        for n in reversed(range(STEPS)):
            at = jnp.where(sched[SENT[n] - 1, lane] == b, n, at)
        tab[FIRST + b] = at
    for b in range(NB):
        ahead = jnp.int32(0)
        for e in range(NB):
            ahead = ahead + jnp.where(tab[FIRST + e] < tab[FIRST + b], 1, 0)
        tab[TURN + b] = ahead
    for n in range(NB):
        found = jnp.int32(0)
        for b in range(NB):
            found = jnp.where(tab[TURN + b] == n, b, found)
        tab[BLOCK + n] = found
        tab[OFFER + n] = tab[TURN + sched[SENT[n] - 1, lane]]
    pairs[...] = jnp.zeros_like(pairs)

    def widen_all(wide):
        def body(r, c):
            widen(raw.at[r], wide.at[r])
            return c

        lax.fori_loop(0, NREL, body, 0)

    load_att.wait()
    widen_all(att_wide)
    load_msg.start()
    for rt in range(2):
        for way in range(2):
            first(rt, way, 0).wait_recv()
            forward(rt, way).start()

    load_wq.wait()

    def ask_query(n, c):
        b = tab[BLOCK + n]
        rows = jnp.concatenate([near0[0, b], near0[1, b]], axis=0)
        turned[n] = dot(rows, wqo[tab[OTYPE + b]]).astype(BF).T
        return c

    lax.fori_loop(0, NB, ask_query, 0)
    load_wo.start()
    load_msg.wait()
    widen_all(msg_wide)
    load_wk.wait()
    load_wv.wait()
    relay(0)
    for rt in range(2):
        for way in range(2):
            first(rt, way, 1).wait_recv()
    pick(1, last=1)
    pick(3, last=3)
    for rt in range(2):
        for way in range(2):
            forward(rt, way).wait_recv()
    pick(2)

    def part_of(rt, i):
        rows = held[rt, jnp.clip(i - 32, 0, 35)]
        for o in range(RING):
            rows = jnp.where(i // NB == o, near[o][rt, jnp.clip(i - o * NB, 0, NB - 1)], rows)
        return rows

    def transform(n, c):
        p = tab[ORDER + n]
        src = jnp.concatenate(
            [part_of(0, tab[IDX + p]), part_of(1, tab[IDX + REQ + p])], axis=0
        )
        ts = tab[STYPE + p]
        r = tab[RELA + p]
        key = dot(src, wks[ts]).astype(BF)
        keyed[n] = spread(key, att_wide.at[r]).astype(BF)
        value = dot(src, wvs[ts]).astype(BF)
        message[n] = spread(value, msg_wide.at[r]).astype(BF).T
        return c

    def transform_all(start, stop):
        def two(i, c):
            transform(2 * i, c)
            return transform(2 * i + 1, c)

        lax.fori_loop(start // 2, stop // 2, two, 0)

    take(3, 0)
    take(1, 0)
    take(2, 0)
    relay(3)
    transform_all(0, READY[0])
    relay(1)
    for rt in range(2):
        second(rt, 1, 1).start()
    relay(2)
    for rt in range(2):
        second(rt, 3, 3).start()
    take(3, 1)
    take(1, 3)
    transform_all(READY[0], READY[1])
    take(3, 2)
    take(2, 3)
    transform_all(READY[1], READY[2])
    take(1, 2)
    take(2, 1)
    take(2, 2)
    transform_all(READY[2], READY[3])
    take(1, 1)
    take(3, 3)
    transform_all(READY[3], READY[4])

    for rt in range(2):
        for way in range(2):
            for part in range(2):
                first(rt, way, part).wait_send()
            forward(rt, way).wait_send()
        for o in range(4):
            for d in (1, 2, 3):
                second(rt, d, o).wait_send()
            onward(rt, o).wait_send()
    load_wo.wait()

    load_pos = [
        pltpu.make_async_copy(
            pos.at[:, pl.ds(rt * HALF, HALF), :], far.at[rt, pl.ds(0, NB)], lsem.at[rt]
        )
        for rt in range(2)
    ]
    for c in load_pos:
        c.start()

    left = lax.broadcasted_iota(jnp.int32, (1, WIN), 1) < TILE
    unit = math.log2(math.e) / math.sqrt(DH)

    def attend(n, c):
        b = tab[BLOCK + n]
        where = [tab[PLACE + b * NT + j] for j in range(NT)]
        rel = [tab[RELA + b * NT + j] for j in range(NT)]
        for h in range(HEADS):
            lo = h * DH - PAIR[h // 2]
            pairs[h // 2, lo : lo + DH, h % 2 * TILE : (h % 2 + 1) * TILE] = turned[
                n, h * DH : (h + 1) * DH, :
            ]
        for q in range(HEADS // 2):
            w = PAIR[q]
            scores = []
            for j in range(NT):
                scale = jnp.where(left, prior[rel[j], 2 * q], prior[rel[j], 2 * q + 1]) * unit
                scores.append(dot(keyed[where[j], :, w : w + WIN], pairs[q]) * scale)
            top = jnp.maximum(
                jnp.maximum(scores[0], scores[1]), jnp.maximum(scores[2], scores[3])
            )
            top = jnp.max(top, axis=0, keepdims=True)
            weights = [jnp.exp2(s - top) for s in scores]
            total = jnp.sum(
                (weights[0] + weights[1]) + (weights[2] + weights[3]), axis=0, keepdims=True
            )
            inv = 1.0 / total
            rows = slice(2 * q * DH, (2 * q + 2) * DH)
            lhs = jnp.concatenate([message[where[j], rows, :] for j in range(NT)], axis=1)
            got = dot(lhs, jnp.concatenate([e.astype(BF) for e in weights], axis=0))
            agg[2 * q * DH : (2 * q + 1) * DH, :] = got[:DH, :TILE] * inv[:, :TILE]
            agg[(2 * q + 1) * DH : (2 * q + 2) * DH, :] = got[DH:, TILE:] * inv[:, TILE:]
        merged = agg[...]
        active = (0.5 * merged * (1.0 + lax.erf(merged * math.sqrt(0.5)))).astype(BF).T
        tb = tab[OTYPE + b]
        projected = dot(active, wqo[tb])
        a = jax.nn.sigmoid(jnp.full((1, D), gate[tb], F32))
        own = jnp.concatenate([near0[0, b], near0[1, b]], axis=0).astype(F32)
        emb = (a * projected + (1.0 - a) * own).astype(BF)
        held[0, n] = emb[:HALF]
        held[1, n] = emb[HALF:]
        turned[n] = emb.T

    def give(step):
        return pltpu.make_async_remote_copy(
            src_ref=send.at[0, pl.ds(2 * SENT.index(step), 2)],
            dst_ref=negs.at[step - 1],
            send_sem=s3.at[step - 1],
            recv_sem=r3.at[step - 1],
            device_id=lane_id(step),
            device_id_type=MESH,
        )

    def to_via(step):
        return pltpu.make_async_remote_copy(
            src_ref=send.at[0, pl.ds(2 * SENT.index(step), 2)],
            dst_ref=via.at[8 - step],
            send_sem=s3.at[step - 1],
            recv_sem=r4.at[8 - step],
            device_id={"narrow_0": (z + 3) % RING, "narrow_1": (x + step) % RING},
            device_id_type=MESH,
        )

    def from_via(step):
        return pltpu.make_async_remote_copy(
            src_ref=via.at[8 - step],
            dst_ref=negs.at[step - 1],
            send_sem=s4.at[8 - step],
            recv_sem=r3.at[step - 1],
            device_id=to(1, 3),
            device_id_type=MESH,
        )

    def one_block(n, c):
        attend(n, c)
        turn_of = tab[OFFER + n]
        send[0, 2 * n] = held[0, turn_of]
        send[0, 2 * n + 1] = held[1, turn_of]
        for i, step in enumerate(SENT):
            if step == 8:

                @pl.when(n == i)
                def _():
                    to_via(8).start()

                @pl.when(n == i + 3)
                def _():
                    to_via(8).wait_recv()
                    from_via(8).start()

            elif step == 7:

                @pl.when(jnp.logical_and(n == i, x > 0))
                def _():
                    to_via(7).start()

                @pl.when(jnp.logical_and(n == i, x == 0))
                def _():
                    give(7).start()

                @pl.when(jnp.logical_and(n == i + 3, x < RING - 1))
                def _():
                    to_via(7).wait_recv()
                    from_via(7).start()

            else:

                @pl.when(n == i)
                def _(step=step):
                    give(step).start()

        return c

    lax.fori_loop(0, NB, one_block, 0)

    for b in range(NB):
        for rt in range(2):
            send[1, 2 * b + rt] = held[rt, tab[TURN + b]]
    done = [
        pltpu.make_async_copy(
            send.at[1, pl.ds(2 * b + rt, 1)],
            out.at[pl.ds(b, 1), pl.ds(rt * HALF, HALF), :],
            esem.at[2 * b + rt],
        )
        for b in range(NB)
        for rt in range(2)
    ]
    for c in done:
        c.start()
    for c in load_pos:
        c.wait()

    scale = 1.0 / math.sqrt(D)
    for b in range(NB):
        turn_of = tab[TURN + b]
        fold = jnp.zeros((TILE, TILE), F32)
        own = jnp.concatenate([held[0, turn_of], held[1, turn_of]], axis=0).astype(F32)
        near_by = jnp.concatenate([far[0, b], far[1, b]], axis=0).astype(F32)
        prod = own * near_by
        for k in range(D // TILE):
            fold = fold + prod[:, k * TILE : (k + 1) * TILE]
        row = jnp.sum(fold.T, axis=0, keepdims=True) * scale
        positive[b] = jnp.broadcast_to(row, (8, TILE))

    own_type = [tab[OTYPE + tab[BLOCK + n]] for n in range(NB)]
    base = [
        jnp.concatenate(
            [positive[tab[BLOCK + n]][0:1], positive[tab[BLOCK + n + 1]][0:1]],
            axis=1,
        )
        for n in range(0, NB, 2)
    ]

    def against(s, state):
        frm = (lane + LANES - s - 1) % LANES
        kind = types[frm * NB + sched[s, frm]]
        both = jnp.concatenate([negs[s, 0], negs[s, 1]], axis=0)
        new = []
        for m in range(NB // 2):
            high, den = state[2 * m], state[2 * m + 1]
            emb = jnp.concatenate([turned[2 * m], turned[2 * m + 1]], axis=1)
            even = jnp.where(own_type[2 * m] == kind, 0.0, -jnp.inf)
            odd = jnp.where(own_type[2 * m + 1] == kind, 0.0, -jnp.inf)
            v = dot(both, emb) * scale + jnp.where(left, even, odd)
            top = jnp.maximum(high, jnp.max(v, axis=0, keepdims=True))
            den = den * jnp.exp(high - top) + jnp.sum(jnp.exp(v - top), axis=0, keepdims=True)
            new += [top, den]
        return tuple(new)

    state = []
    for m in range(NB // 2):
        state += [base[m], jnp.ones((1, WIN), F32)]
    for step in (4, 5, 8, 6, 3, 7, 2, 1):
        give(step).wait_recv()
        state = against(step - 1, state)

    total = jnp.zeros((1, TILE), F32)
    for m in range(NB // 2):
        row = state[2 * m] + jnp.log(state[2 * m + 1]) - base[m]
        for i in range(2):
            n = 2 * m + i
            one = row[:, i * TILE : (i + 1) * TILE]
            total = total + one * weight[own_type[n]]
            rows_of[n] = jnp.broadcast_to(one, (8, TILE))
    subtotal[...] = jnp.broadcast_to(total, (8, TILE))

    def lane_copy(by):
        return pltpu.make_async_remote_copy(
            src_ref=subtotal,
            dst_ref=lanes.at[by],
            send_sem=sl.at[by],
            recv_sem=rl.at[by],
            device_id=lane_id(by),
            device_id_type=MESH,
        )

    for by in range(1, LANES):
        lane_copy(by).start()
    for b in range(NB):
        loss[b : b + 1, :] = rows_of[tab[TURN + b]][0:1]
    lanes[0] = subtotal[...]
    for by in range(1, LANES):
        lane_copy(by).wait_recv()
    acc = lanes[lane]
    for k in range(1, LANES):
        acc = acc + lanes[(lane + LANES - k) % LANES]
    doms[0] = acc

    def dom_copy(by):
        return pltpu.make_async_remote_copy(
            src_ref=doms.at[0],
            dst_ref=doms.at[by],
            send_sem=sd.at[by],
            recv_sem=rd.at[by],
            device_id=dom_id(by),
            device_id_type=MESH,
        )

    for by in range(1, 8):
        dom_copy(by).start()
    for c in done:
        c.wait()
    for step in SENT:
        give(step).wait_send()
    from_via(8).wait_send()

    @pl.when(x < RING - 1)
    def _():
        from_via(7).wait_send()

    for by in range(1, LANES):
        lane_copy(by).wait_send()
    for by in range(1, 8):
        dom_copy(by).wait_recv()
    acc = doms[dom]
    for k in range(1, 8):
        acc = acc + doms[(dom + 8 - k) % 8]
    whole = jnp.sum(acc, axis=1, keepdims=True) * (1.0 / (NB * TILE * 128))
    mean[...] = jnp.broadcast_to(whole, (8, TILE))
    for by in range(1, 8):
        dom_copy(by).wait_send()


def layer(*operands):
    smem = pl.BlockSpec(memory_space=pltpu.SMEM)
    vmem = pl.BlockSpec(memory_space=pltpu.VMEM)
    hbm = pl.BlockSpec(memory_space=pl.ANY)
    dma = pltpu.SemaphoreType.DMA
    return pl.pallas_call(
        layer_kernel,
        name="layer",
        out_shape=(
            jax.ShapeDtypeStruct((NB, TILE, D), BF),
            jax.ShapeDtypeStruct((NB, TILE), F32),
            jax.ShapeDtypeStruct((8, TILE), F32),
        ),
        in_specs=[smem] * 7 + [hbm] * 8,
        out_specs=(hbm, vmem, vmem),
        scratch_shapes=[
            pltpu.SMEM((TABLE,), jnp.int32),
            *[pltpu.VMEM((2, NB, HALF, D), BF)] * 4,
            pltpu.VMEM((2, 36, HALF, D), BF),
            pltpu.VMEM((2, 36, HALF, D), BF),
            pltpu.VMEM((2, 36, HALF, D), BF),
            pltpu.VMEM((2, 12, HALF, D), BF),
            pltpu.VMEM((3, D, D), BF),
            pltpu.VMEM((3, D, D), BF),
            pltpu.VMEM((3, D, D), BF),
            pltpu.VMEM((NREL, D, DH), BF),
            pltpu.VMEM((NREL, STRIPS, WIN), BF),
            pltpu.VMEM((NREL, STRIPS, WIN), BF),
            pltpu.VMEM((NB, D, TILE), BF),
            pltpu.VMEM((REQ, TILE, D), BF),
            pltpu.VMEM((REQ, D, TILE), BF),
            pltpu.VMEM((HEADS // 2, WIN, WIN), BF),
            pltpu.VMEM((D, TILE), F32),
            pltpu.VMEM((STEPS, 2, HALF, D), BF),
            pltpu.VMEM((2, 2, HALF, D), BF),
            pltpu.VMEM((NB, 8, TILE), F32),
            pltpu.VMEM((NB, 8, TILE), F32),
            pltpu.VMEM((8, TILE), F32),
            pltpu.VMEM((LANES, 8, TILE), F32),
            pltpu.VMEM((8, 8, TILE), F32),
            dma((2,)),
            dma((6,)),
            dma((2 * NB,)),
            dma((2, 2, 3)),
            dma((2, 2, 3)),
            dma((2, 4, 4)),
            dma((2, 4, 4)),
            dma((STEPS,)),
            dma((STEPS,)),
            dma((2,)),
            dma((2,)),
            dma((LANES,)),
            dma((LANES,)),
            dma((8,)),
            dma((8,)),
        ],
        compiler_params=pltpu.CompilerParams(
            collective_id=0, has_side_effects=True, vmem_limit_bytes=67043328
        ),
    )(*operands)


def finish_kernel(emb, loss, mean, emb_out, loss_out, mean_out, buf, came, went):
    def come(i):
        return pltpu.make_async_copy(emb.at[i], buf.at[i], came.at[i])

    def go(i):
        return pltpu.make_async_copy(buf.at[i], emb_out.at[i], went.at[i])

    for i in range(NB):
        come(i).start()
    loss_out[...] = loss[...]
    mean_out[...] = mean[0:1, 0:1]
    for i in range(NB):
        come(i).wait()
        go(i).start()
    for i in range(NB):
        go(i).wait()


def finish(emb, loss, mean):
    vmem = pl.BlockSpec(memory_space=pltpu.VMEM)
    hbm = pl.BlockSpec(memory_space=pl.ANY)
    return pl.pallas_call(
        finish_kernel,
        name="finish",
        out_shape=(
            jax.ShapeDtypeStruct((NB, TILE, D), BF),
            jax.ShapeDtypeStruct((NB, TILE), F32),
            jax.ShapeDtypeStruct((1, 1), F32),
        ),
        in_specs=[hbm, vmem, vmem],
        out_specs=(hbm, vmem, vmem),
        scratch_shapes=[
            pltpu.VMEM((NB, TILE, D), BF),
            pltpu.SemaphoreType.DMA((NB,)),
            pltpu.SemaphoreType.DMA((NB,)),
        ],
    )(emb, loss, mean)


def shards(
    feats,
    node_type,
    tiles,
    relation,
    neg_sched,
    w_query,
    w_key,
    w_value,
    w_out,
    rel_att,
    rel_msg,
    rel_prior,
    skip_gate,
    pos_view,
    type_weight,
):
    blocks = feats.reshape(NB, TILE, D)
    emb, loss, mean = layer(
        tiles.T,
        node_type,
        relation.T,
        neg_sched.T,
        rel_prior,
        skip_gate,
        type_weight,
        blocks,
        pos_view.reshape(NB, TILE, D),
        w_query,
        w_key,
        w_value,
        w_out,
        rel_att.reshape(NREL, D, DH),
        rel_msg.reshape(NREL, D, DH),
    )
    emb, loss, mean = finish(emb, loss, mean)
    return emb.reshape(NB * TILE, D), loss.reshape(NB * TILE), mean[0, 0]


def solution(mesh):
    finer = Mesh(mesh.devices.reshape(4, 2, 4, 4), DOM_NARROW)
    in_specs = (
        P(DOM_NARROW, None),
        P(DOM),
        P(DOM, None),
        P(DOM_NARROW, None),
        P(DOM, None),
        P(),
        P(),
        P(),
        P(),
        P(),
        P(),
        P(),
        P(),
        P(DOM_NARROW, None),
        P(),
    )
    out_specs = (P(DOM_NARROW, None), P(DOM_NARROW), P())
    return jax.shard_map(
        shards, mesh=finer, in_specs=in_specs, out_specs=out_specs, check_vma=False
    )
```

```python
import functools
import math

import jax
import jax.numpy as jnp
from jax import lax
from jax.experimental import pallas as pl
from jax.experimental.pallas import tpu as pltpu
from jax.sharding import Mesh
from jax.sharding import PartitionSpec as P

D = 768
HEADS = 8
DH = 96
TILE = 128
HALF = TILE // 2
NT = 4
NB = 8
REQ = NB * NT
RING = 4
CAP = 3
NREL = 5
STEPS = 8
LANES = 16
WIN = 256
STRIP = [(0, 384), (128, 640), (384, 768)]
DOM_NARROW = ("dom_0", "dom_1", "narrow_0", "narrow_1")
DOM = ("dom_0", "dom_1")
MESH = pl.DeviceIdType.MESH
BF = jnp.bfloat16
F32 = jnp.float32

SEL = 0
IDX = 72
STYPE = 136
RELA = 168
PLACE = 200
ORDER = 232
STAGE = 264
OTYPE = 296
FIRST = 304
TURN = 312
BLOCK = 320
OFFER = 328
TABLE = 336
SENT = (4, 8, 5, 7, 6, 3, 2, 1)
READY = [4, 10, 16, 26, 32]
STAGE_OF = {
    (1, 3): 1, (3, 1): 1, (2, 3): 2, (3, 2): 2, (1, 2): 3, (2, 1): 3, (2, 2): 3, (1, 1): 4, (3, 3): 4,
}
STRIP_AT = [0, 384, 896]
STRIPS = 1280
PAIR = [0, 128, 384, 512]


def dot(a, b):
    return jnp.dot(a, b, preferred_element_type=F32)


def dot_t(a, b):
    return lax.dot_general(a, b, (((1,), (1,)), ((), ())), preferred_element_type=F32)


def head_of(index):
    return sum((index >= DH * h).astype(jnp.int32) for h in range(1, HEADS))


def widen(rel, wide):
    for c, (lo, hi) in enumerate(STRIP):
        col = lax.broadcasted_iota(jnp.int32, (DH, WIN), 1) + c * WIN
        row = lax.broadcasted_iota(jnp.int32, (DH, WIN), 0)
        place = (col - DH * head_of(col) == row).astype(F32).astype(BF)
        full = dot(rel[lo:hi, :], place)
        col = lax.broadcasted_iota(jnp.int32, (hi - lo, WIN), 1) + c * WIN
        row = lax.broadcasted_iota(jnp.int32, (hi - lo, WIN), 0) + lo
        full = jnp.where(head_of(row) == head_of(col), full, 0.0)
        wide[STRIP_AT[c] : STRIP_AT[c] + hi - lo, :] = full.astype(BF)


def spread(rows, wide):
    return jnp.concatenate(
        [
            dot(rows[:, lo:hi], wide[STRIP_AT[c] : STRIP_AT[c] + hi - lo, :])
            for c, (lo, hi) in enumerate(STRIP)
        ],
        axis=1,
    )


def layer_kernel(
    tiles, types, relation, sched, prior, gate, weight, feats, pos, wq, wk, wv, wo, att, msg,
    out, loss, mean,
    tab, near0, near1, near2, near3, far, held, send, transit,
    wqo, wks, wvs, raw, att_wide, msg_wide, turned, keyed, message, pairs, agg,
    negs, via, positive, rows_of, subtotal, lanes, doms,
    lsem, wsem, esem, s1, r1, s2, r2, s3, r3, s4, r4, sl, rl, sd, rd,
):
    z = lax.axis_index("narrow_0")
    x = lax.axis_index("narrow_1")
    lane = z * RING + x
    coord = [x, z]
    name = ["narrow_1", "narrow_0"]
    near = [near0, near1, near2, near3]

    def to(axis, by):
        return {name[axis]: (coord[axis] + by) % RING}

    local = [
        pltpu.make_async_copy(feats.at[:, pl.ds(rt * HALF, HALF), :], near0.at[rt], lsem.at[rt])
        for rt in range(2)
    ]
    for c in local:
        c.start()
    dom = lax.axis_index("dom_0") * 2 + lax.axis_index("dom_1")

    def lane_id(by):
        other = (lane + by) % LANES
        return {"narrow_0": other // RING, "narrow_1": other % RING}

    def dom_id(by):
        other = (dom + by) % 8
        return {"dom_0": other // 2, "dom_1": other % 2}

    barrier = pltpu.get_barrier_semaphore()
    for by in range(1, LANES):
        pl.semaphore_signal(barrier, 1, device_id=lane_id(by), device_id_type=MESH)
    for by in range(1, 8):
        pl.semaphore_signal(barrier, 1, device_id=dom_id(by), device_id_type=MESH)
    pl.semaphore_wait(barrier, LANES - 1 + 7)

    def first(rt, way, part):
        by = slot = (1, 3)[way]
        half = part if way == 0 else 1 - part
        return pltpu.make_async_remote_copy(
            src_ref=feats.at[pl.ds(half * 4, 4), pl.ds(rt * HALF, HALF), :],
            dst_ref=near[slot].at[rt, pl.ds(half * 4, 4)],
            send_sem=s1.at[rt, way, part],
            recv_sem=r1.at[rt, way, part],
            device_id=to(rt, by),
            device_id_type=MESH,
        )

    def forward(rt, way):
        by = slot = (1, 3)[way]
        return pltpu.make_async_remote_copy(
            src_ref=near[slot].at[rt, pl.ds(way * 4, 4)],
            dst_ref=near2.at[rt, pl.ds(way * 4, 4)],
            send_sem=s1.at[rt, way, 2],
            recv_sem=r1.at[rt, way, 2],
            device_id=to(rt, by),
            device_id_type=MESH,
        )

    def second(rt, d, o):
        at = pl.ds((d - 1) * 12 + o * CAP, CAP)
        if d == 2:
            dst = transit.at[rt, pl.ds(o * CAP, CAP)]
            by = 1 if o < 2 else 3
        else:
            dst = far.at[rt, at]
            by = d
        return pltpu.make_async_remote_copy(
            src_ref=send.at[rt, at],
            dst_ref=dst,
            send_sem=s2.at[rt, d - 1, o],
            recv_sem=r2.at[rt, d - 1, o],
            device_id=to(1 - rt, by),
            device_id_type=MESH,
        )

    def onward(rt, o):
        return pltpu.make_async_remote_copy(
            src_ref=transit.at[rt, pl.ds(o * CAP, CAP)],
            dst_ref=far.at[rt, pl.ds(12 + o * CAP, CAP)],
            send_sem=s2.at[rt, 3, o],
            recv_sem=r2.at[rt, 3, o],
            device_id=to(1 - rt, 1 if o < 2 else 3),
            device_id_type=MESH,
        )

    def pick(o, last=0):
        for d in (2, 1, 3):
            for rt in range(2):
                for k in range(CAP):
                    at = (d - 1) * 12 + o * CAP + k
                    send[rt, at] = near[o][rt, tab[SEL + rt * 36 + at]]
                if d != last:
                    second(rt, d, o).start()

    def take(d, o):
        at = (d - 1) * 12 + o * CAP
        for rt in range(2):
            (onward(rt, o) if d == 2 else second(rt, d, o)).wait_recv()
            held[rt, at : at + CAP] = far[rt, at : at + CAP]

    def relay(o):
        for rt in range(2):
            second(rt, 2, o).wait_recv()
            onward(rt, o).start()

    for part in range(2):
        for rt in range(2):
            for way in range(2):
                first(rt, way, part).start()
    load_wq = pltpu.make_async_copy(wq, wqo, wsem.at[0])
    load_wk = pltpu.make_async_copy(wk, wks, wsem.at[1])
    load_wv = pltpu.make_async_copy(wv, wvs, wsem.at[2])
    load_att = pltpu.make_async_copy(att, raw, wsem.at[3])
    load_msg = pltpu.make_async_copy(msg, raw, wsem.at[4])
    load_wo = pltpu.make_async_copy(wo, wqo, wsem.at[5])
    load_att.start()
    load_wq.start()
    load_wk.start()
    load_wv.start()

    for rt in range(2):
        for d in range(1, RING):
            if rt == 0:
                dst = (z + d) % RING * RING + x
            else:
                dst = z * RING + (x + d) % RING

            def ask(p, c, rt=rt, dst=dst):
                c = list(c)
                t = tiles[p % NT, dst * NB + p // NT]
                owner = t // NB
                oz = (z - owner // RING + RING) % RING
                ox = (x - owner % RING + RING) % RING
                here, o = (oz, ox) if rt == 0 else (ox, oz)
                for i in range(RING):
                    hit = jnp.logical_and(here == 0, o == i)
                    c[i] = jnp.where(hit, c[i] + c[RING + i] * (t % NB), c[i])
                    c[RING + i] = jnp.where(hit, c[RING + i] * NB, c[RING + i])
                return tuple(c)

            got = lax.fori_loop(
                0, REQ, ask, (jnp.int32(0),) * RING + (jnp.int32(1),) * RING
            )
            for o in range(RING):
                for k in range(CAP):
                    tab[SEL + rt * 36 + (d - 1) * 12 + o * CAP + k] = (
                        got[o] // NB**k
                    ) % NB
    for c in local:
        c.wait()
    pick(0)

    def mine(p, c):
        c = list(c)
        t = tiles[p % NT, lane * NB + p // NT]
        owner = t // NB
        oz = (z - owner // RING + RING) % RING
        ox = (x - owner % RING + RING) % RING
        back = oz * RING + ox
        k = jnp.int32(0)
        for i in range(LANES):
            hit = back == i
            k = jnp.where(hit, c[i], k)
            c[i] = jnp.where(hit, c[i] + 1, c[i])
        stage = jnp.int32(0)
        for (a, b), v in STAGE_OF.items():
            stage = jnp.where(back == a * RING + b, v, stage)
        tab[IDX + p] = jnp.where(
            oz == 0, ox * NB + t % NB, 32 + (oz - 1) * 12 + ox * CAP + k
        )
        tab[IDX + REQ + p] = jnp.where(
            ox == 0, oz * NB + t % NB, 32 + (ox - 1) * 12 + oz * CAP + k
        )
        tab[STYPE + p] = types[t]
        tab[RELA + p] = relation[p % NT, p // NT]
        tab[STAGE + p] = stage
        for v in range(4):
            c[LANES + v] = c[LANES + v] + jnp.where(stage <= v, 1, 0)
        return tuple(c)

    counts = lax.fori_loop(0, REQ, mine, (jnp.int32(0),) * (LANES + 4))[LANES:]

    def turn(p, c):
        c = list(c)
        stage = tab[STAGE + p]
        place = jnp.int32(0)
        for v in range(5):
            hit = stage == v
            place = jnp.where(hit, c[v], place)
            c[v] = jnp.where(hit, c[v] + 1, c[v])
        tab[PLACE + p] = place
        return tuple(c)

    lax.fori_loop(0, REQ, turn, (jnp.int32(0),) + tuple(counts))

    def invert(n, c):
        found = jnp.int32(0)
        for p in range(REQ):
            found = jnp.where(tab[PLACE + p] == n, p, found)
        tab[ORDER + n] = found
        return c

    lax.fori_loop(0, REQ, invert, 0)
    for b in range(NB):
        tab[OTYPE + b] = types[lane * NB + b]
        at = jnp.int32(STEPS + b)
        for n in reversed(range(STEPS)):
            at = jnp.where(sched[SENT[n] - 1, lane] == b, n, at)
        tab[FIRST + b] = at
    for b in range(NB):
        ahead = jnp.int32(0)
        for e in range(NB):
            ahead = ahead + jnp.where(tab[FIRST + e] < tab[FIRST + b], 1, 0)
        tab[TURN + b] = ahead
    for n in range(NB):
        found = jnp.int32(0)
        for b in range(NB):
            found = jnp.where(tab[TURN + b] == n, b, found)
        tab[BLOCK + n] = found
        tab[OFFER + n] = tab[TURN + sched[SENT[n] - 1, lane]]
    pairs[...] = jnp.zeros_like(pairs)

    def widen_all(wide):
        def body(r, c):
            widen(raw.at[r], wide.at[r])
            return c

        lax.fori_loop(0, NREL, body, 0)

    load_att.wait()
    widen_all(att_wide)
    load_msg.start()
    for rt in range(2):
        for way in range(2):
            first(rt, way, 0).wait_recv()
            forward(rt, way).start()

    load_wq.wait()

    def ask_query(n, c):
        b = tab[BLOCK + n]
        rows = jnp.concatenate([near0[0, b], near0[1, b]], axis=0)
        turned[n] = dot(rows, wqo[tab[OTYPE + b]]).astype(BF).T
        return c

    lax.fori_loop(0, NB, ask_query, 0)
    load_wo.start()
    load_msg.wait()
    widen_all(msg_wide)
    load_wk.wait()
    load_wv.wait()
    relay(0)
    for rt in range(2):
        for way in range(2):
            first(rt, way, 1).wait_recv()
    pick(1, last=1)
    pick(3, last=3)
    for rt in range(2):
        for way in range(2):
            forward(rt, way).wait_recv()
    pick(2)

    def part_of(rt, i):
        rows = held[rt, jnp.clip(i - 32, 0, 35)]
        for o in range(RING):
            rows = jnp.where(i // NB == o, near[o][rt, jnp.clip(i - o * NB, 0, NB - 1)], rows)
        return rows

    def transform(n, c):
        p = tab[ORDER + n]
        src = jnp.concatenate(
            [part_of(0, tab[IDX + p]), part_of(1, tab[IDX + REQ + p])], axis=0
        )
        ts = tab[STYPE + p]
        r = tab[RELA + p]
        key = dot(src, wks[ts]).astype(BF)
        keyed[n] = spread(key, att_wide.at[r]).astype(BF)
        value = dot(src, wvs[ts]).astype(BF)
        message[n] = spread(value, msg_wide.at[r]).astype(BF).T
        return c

    def transform_all(start, stop):
        def two(i, c):
            transform(2 * i, c)
            return transform(2 * i + 1, c)

        lax.fori_loop(start // 2, stop // 2, two, 0)

    take(3, 0)
    take(1, 0)
    take(2, 0)
    relay(3)
    transform_all(0, READY[0])
    relay(1)
    for rt in range(2):
        second(rt, 1, 1).start()
    relay(2)
    for rt in range(2):
        second(rt, 3, 3).start()
    take(3, 1)
    take(1, 3)
    transform_all(READY[0], READY[1])
    take(3, 2)
    take(2, 3)
    transform_all(READY[1], READY[2])
    take(1, 2)
    take(2, 1)
    take(2, 2)
    transform_all(READY[2], READY[3])
    take(1, 1)
    take(3, 3)
    transform_all(READY[3], READY[4])

    for rt in range(2):
        for way in range(2):
            for part in range(2):
                first(rt, way, part).wait_send()
            forward(rt, way).wait_send()
        for o in range(4):
            for d in (1, 2, 3):
                second(rt, d, o).wait_send()
            onward(rt, o).wait_send()
    load_wo.wait()

    load_pos = [
        pltpu.make_async_copy(
            pos.at[:, pl.ds(rt * HALF, HALF), :], far.at[rt, pl.ds(0, NB)], lsem.at[rt]
        )
        for rt in range(2)
    ]
    for c in load_pos:
        c.start()

    left = lax.broadcasted_iota(jnp.int32, (1, WIN), 1) < TILE
    unit = math.log2(math.e) / math.sqrt(DH)

    def attend(n, c):
        b = tab[BLOCK + n]
        where = [tab[PLACE + b * NT + j] for j in range(NT)]
        rel = [tab[RELA + b * NT + j] for j in range(NT)]
        for h in range(HEADS):
            lo = h * DH - PAIR[h // 2]
            pairs[h // 2, lo : lo + DH, h % 2 * TILE : (h % 2 + 1) * TILE] = turned[
                n, h * DH : (h + 1) * DH, :
            ]
        for q in range(HEADS // 2):
            w = PAIR[q]
            scores = []
            for j in range(NT):
                scale = jnp.where(left, prior[rel[j], 2 * q], prior[rel[j], 2 * q + 1]) * unit
                scores.append(dot(keyed[where[j], :, w : w + WIN], pairs[q]) * scale)
            top = jnp.maximum(
                jnp.maximum(scores[0], scores[1]), jnp.maximum(scores[2], scores[3])
            )
            top = jnp.max(top, axis=0, keepdims=True)
            weights = [jnp.exp2(s - top) for s in scores]
            total = jnp.sum(
                (weights[0] + weights[1]) + (weights[2] + weights[3]), axis=0, keepdims=True
            )
            inv = 1.0 / total
            rows = slice(2 * q * DH, (2 * q + 2) * DH)
            lhs = jnp.concatenate([message[where[j], rows, :] for j in range(NT)], axis=1)
            got = dot(lhs, jnp.concatenate([e.astype(BF) for e in weights], axis=0))
            agg[2 * q * DH : (2 * q + 1) * DH, :] = got[:DH, :TILE] * inv[:, :TILE]
            agg[(2 * q + 1) * DH : (2 * q + 2) * DH, :] = got[DH:, TILE:] * inv[:, TILE:]
        merged = agg[...]
        active = (0.5 * merged * (1.0 + lax.erf(merged * math.sqrt(0.5)))).astype(BF).T
        tb = tab[OTYPE + b]
        projected = dot(active, wqo[tb])
        a = jax.nn.sigmoid(jnp.full((1, D), gate[tb], F32))
        own = jnp.concatenate([near0[0, b], near0[1, b]], axis=0).astype(F32)
        emb = (a * projected + (1.0 - a) * own).astype(BF)
        held[0, n] = emb[:HALF]
        held[1, n] = emb[HALF:]
        turned[n] = emb.T

    def give(step):
        return pltpu.make_async_remote_copy(
            src_ref=send.at[0, pl.ds(2 * SENT.index(step), 2)],
            dst_ref=negs.at[step - 1],
            send_sem=s3.at[step - 1],
            recv_sem=r3.at[step - 1],
            device_id=lane_id(step),
            device_id_type=MESH,
        )

    def to_via(step):
        return pltpu.make_async_remote_copy(
            src_ref=send.at[0, pl.ds(2 * SENT.index(step), 2)],
            dst_ref=via.at[8 - step],
            send_sem=s3.at[step - 1],
            recv_sem=r4.at[8 - step],
            device_id={"narrow_0": (z + 3) % RING, "narrow_1": (x + step) % RING},
            device_id_type=MESH,
        )

    def from_via(step):
        return pltpu.make_async_remote_copy(
            src_ref=via.at[8 - step],
            dst_ref=negs.at[step - 1],
            send_sem=s4.at[8 - step],
            recv_sem=r3.at[step - 1],
            device_id=to(1, 3),
            device_id_type=MESH,
        )

    def one_block(n, c):
        attend(n, c)
        turn_of = tab[OFFER + n]
        send[0, 2 * n] = held[0, turn_of]
        send[0, 2 * n + 1] = held[1, turn_of]
        for i, step in enumerate(SENT):
            if step == 8:

                @pl.when(n == i)
                def _():
                    to_via(8).start()

                @pl.when(n == i + 3)
                def _():
                    to_via(8).wait_recv()
                    from_via(8).start()

            elif step == 7:

                @pl.when(jnp.logical_and(n == i, x > 0))
                def _():
                    to_via(7).start()

                @pl.when(jnp.logical_and(n == i, x == 0))
                def _():
                    give(7).start()

                @pl.when(jnp.logical_and(n == i + 3, x < RING - 1))
                def _():
                    to_via(7).wait_recv()
                    from_via(7).start()

            else:

                @pl.when(n == i)
                def _(step=step):
                    give(step).start()

        return c

    lax.fori_loop(0, NB, one_block, 0)

    for b in range(NB):
        for rt in range(2):
            send[1, 2 * b + rt] = held[rt, tab[TURN + b]]
    done = [
        pltpu.make_async_copy(
            send.at[1, pl.ds(2 * b + rt, 1)],
            out.at[pl.ds(b, 1), pl.ds(rt * HALF, HALF), :],
            esem.at[2 * b + rt],
        )
        for b in range(NB)
        for rt in range(2)
    ]
    for c in done:
        c.start()
    for c in load_pos:
        c.wait()

    scale = 1.0 / math.sqrt(D)
    for b in range(NB):
        turn_of = tab[TURN + b]
        fold = jnp.zeros((TILE, TILE), F32)
        own = jnp.concatenate([held[0, turn_of], held[1, turn_of]], axis=0).astype(F32)
        near_by = jnp.concatenate([far[0, b], far[1, b]], axis=0).astype(F32)
        prod = own * near_by
        for k in range(D // TILE):
            fold = fold + prod[:, k * TILE : (k + 1) * TILE]
        row = jnp.sum(fold.T, axis=0, keepdims=True) * scale
        positive[b] = jnp.broadcast_to(row, (8, TILE))

    own_type = [tab[OTYPE + tab[BLOCK + n]] for n in range(NB)]
    base = [
        jnp.concatenate(
            [positive[tab[BLOCK + n]][0:1], positive[tab[BLOCK + n + 1]][0:1]],
            axis=1,
        )
        for n in range(0, NB, 2)
    ]

    def against(s, state):
        frm = (lane + LANES - s - 1) % LANES
        kind = types[frm * NB + sched[s, frm]]
        both = jnp.concatenate([negs[s, 0], negs[s, 1]], axis=0)
        new = []
        for m in range(NB // 2):
            high, den = state[2 * m], state[2 * m + 1]
            emb = jnp.concatenate([turned[2 * m], turned[2 * m + 1]], axis=1)
            even = jnp.where(own_type[2 * m] == kind, 0.0, -jnp.inf)
            odd = jnp.where(own_type[2 * m + 1] == kind, 0.0, -jnp.inf)
            v = dot(both, emb) * scale + jnp.where(left, even, odd)
            top = jnp.maximum(high, jnp.max(v, axis=0, keepdims=True))
            den = den * jnp.exp(high - top) + jnp.sum(jnp.exp(v - top), axis=0, keepdims=True)
            new += [top, den]
        return tuple(new)

    state = []
    for m in range(NB // 2):
        state += [base[m], jnp.ones((1, WIN), F32)]
    for step in (4, 5, 8, 6, 3, 7, 2, 1):
        give(step).wait_recv()
        state = against(step - 1, state)

    total = jnp.zeros((1, TILE), F32)
    for m in range(NB // 2):
        row = state[2 * m] + jnp.log(state[2 * m + 1]) - base[m]
        for i in range(2):
            n = 2 * m + i
            one = row[:, i * TILE : (i + 1) * TILE]
            total = total + one * weight[own_type[n]]
            rows_of[n] = jnp.broadcast_to(one, (8, TILE))
    subtotal[...] = jnp.broadcast_to(total, (8, TILE))

    def lane_copy(by):
        return pltpu.make_async_remote_copy(
            src_ref=subtotal,
            dst_ref=lanes.at[by],
            send_sem=sl.at[by],
            recv_sem=rl.at[by],
            device_id=lane_id(by),
            device_id_type=MESH,
        )

    for by in range(1, LANES):
        lane_copy(by).start()
    for b in range(NB):
        loss[b : b + 1, :] = rows_of[tab[TURN + b]][0:1]
    lanes[0] = subtotal[...]
    for by in range(1, LANES):
        lane_copy(by).wait_recv()
    acc = lanes[lane]
    for k in range(1, LANES):
        acc = acc + lanes[(lane + LANES - k) % LANES]
    doms[0] = acc

    def dom_copy(by):
        return pltpu.make_async_remote_copy(
            src_ref=doms.at[0],
            dst_ref=doms.at[by],
            send_sem=sd.at[by],
            recv_sem=rd.at[by],
            device_id=dom_id(by),
            device_id_type=MESH,
        )

    for by in range(1, 8):
        dom_copy(by).start()
    for c in done:
        c.wait()
    for step in SENT:
        give(step).wait_send()
    from_via(8).wait_send()

    @pl.when(x < RING - 1)
    def _():
        from_via(7).wait_send()

    for by in range(1, LANES):
        lane_copy(by).wait_send()
    for by in range(1, 8):
        dom_copy(by).wait_recv()
    acc = doms[dom]
    for k in range(1, 8):
        acc = acc + doms[(dom + 8 - k) % 8]
    whole = jnp.sum(acc, axis=1, keepdims=True) * (1.0 / (NB * TILE * 128))
    mean[...] = jnp.broadcast_to(whole, (8, TILE))
    for by in range(1, 8):
        dom_copy(by).wait_send()


def layer(*operands):
    smem = pl.BlockSpec(memory_space=pltpu.SMEM)
    vmem = pl.BlockSpec(memory_space=pltpu.VMEM)
    hbm = pl.BlockSpec(memory_space=pl.ANY)
    dma = pltpu.SemaphoreType.DMA
    return pl.pallas_call(
        layer_kernel,
        name="layer",
        out_shape=(
            jax.ShapeDtypeStruct((NB, TILE, D), BF),
            jax.ShapeDtypeStruct((NB, TILE), F32),
            jax.ShapeDtypeStruct((8, TILE), F32),
        ),
        in_specs=[smem] * 7 + [hbm] * 8,
        out_specs=(hbm, vmem, vmem),
        scratch_shapes=[
            pltpu.SMEM((TABLE,), jnp.int32),
            *[pltpu.VMEM((2, NB, HALF, D), BF)] * 4,
            pltpu.VMEM((2, 36, HALF, D), BF),
            pltpu.VMEM((2, 36, HALF, D), BF),
            pltpu.VMEM((2, 36, HALF, D), BF),
            pltpu.VMEM((2, 12, HALF, D), BF),
            pltpu.VMEM((3, D, D), BF),
            pltpu.VMEM((3, D, D), BF),
            pltpu.VMEM((3, D, D), BF),
            pltpu.VMEM((NREL, D, DH), BF),
            pltpu.VMEM((NREL, STRIPS, WIN), BF),
            pltpu.VMEM((NREL, STRIPS, WIN), BF),
            pltpu.VMEM((NB, D, TILE), BF),
            pltpu.VMEM((REQ, TILE, D), BF),
            pltpu.VMEM((REQ, D, TILE), BF),
            pltpu.VMEM((HEADS // 2, WIN, WIN), BF),
            pltpu.VMEM((D, TILE), F32),
            pltpu.VMEM((STEPS, 2, HALF, D), BF),
            pltpu.VMEM((2, 2, HALF, D), BF),
            pltpu.VMEM((NB, 8, TILE), F32),
            pltpu.VMEM((NB, 8, TILE), F32),
            pltpu.VMEM((8, TILE), F32),
            pltpu.VMEM((LANES, 8, TILE), F32),
            pltpu.VMEM((8, 8, TILE), F32),
            dma((2,)),
            dma((6,)),
            dma((2 * NB,)),
            dma((2, 2, 3)),
            dma((2, 2, 3)),
            dma((2, 4, 4)),
            dma((2, 4, 4)),
            dma((STEPS,)),
            dma((STEPS,)),
            dma((2,)),
            dma((2,)),
            dma((LANES,)),
            dma((LANES,)),
            dma((8,)),
            dma((8,)),
        ],
        compiler_params=pltpu.CompilerParams(
            collective_id=0, has_side_effects=True, vmem_limit_bytes=67043328
        ),
    )(*operands)


def finish_kernel(emb, loss, mean, emb_out, loss_out, mean_out, buf, came, went):
    def come(i):
        return pltpu.make_async_copy(emb.at[i], buf.at[i], came.at[i])

    def go(i):
        return pltpu.make_async_copy(buf.at[i], emb_out.at[i], went.at[i])

    for i in range(NB):
        come(i).start()
    loss_out[...] = loss[...]
    mean_out[...] = mean[0:1, 0:1]
    for i in range(NB):
        come(i).wait()
        go(i).start()
    for i in range(NB):
        go(i).wait()


def finish(emb, loss, mean):
    vmem = pl.BlockSpec(memory_space=pltpu.VMEM)
    hbm = pl.BlockSpec(memory_space=pl.ANY)
    return pl.pallas_call(
        finish_kernel,
        name="finish",
        out_shape=(
            jax.ShapeDtypeStruct((NB, TILE, D), BF),
            jax.ShapeDtypeStruct((NB, TILE), F32),
            jax.ShapeDtypeStruct((1, 1), F32),
        ),
        in_specs=[hbm, vmem, vmem],
        out_specs=(hbm, vmem, vmem),
        scratch_shapes=[
            pltpu.VMEM((NB, TILE, D), BF),
            pltpu.SemaphoreType.DMA((NB,)),
            pltpu.SemaphoreType.DMA((NB,)),
        ],
    )(emb, loss, mean)


def shards(
    feats,
    node_type,
    tiles,
    relation,
    neg_sched,
    w_query,
    w_key,
    w_value,
    w_out,
    rel_att,
    rel_msg,
    rel_prior,
    skip_gate,
    pos_view,
    type_weight,
):
    blocks = feats.reshape(NB, TILE, D)
    emb, loss, mean = layer(
        tiles.T,
        node_type,
        relation.T,
        neg_sched.T,
        rel_prior,
        skip_gate,
        type_weight,
        blocks,
        pos_view.reshape(NB, TILE, D),
        w_query,
        w_key,
        w_value,
        w_out,
        rel_att.reshape(NREL, D, DH),
        rel_msg.reshape(NREL, D, DH),
    )
    emb, loss, mean = finish(emb, loss, mean)
    return emb.reshape(NB * TILE, D), loss.reshape(NB * TILE), mean[0, 0]


def solution(mesh):
    finer = Mesh(mesh.devices.reshape(4, 2, 4, 4), DOM_NARROW)
    in_specs = (
        P(DOM_NARROW, None),
        P(DOM),
        P(DOM, None),
        P(DOM_NARROW, None),
        P(DOM, None),
        P(),
        P(),
        P(),
        P(),
        P(),
        P(),
        P(),
        P(),
        P(DOM_NARROW, None),
        P(),
    )
    out_specs = (P(DOM_NARROW, None), P(DOM_NARROW), P())
    return jax.shard_map(
        shards, mesh=finer, in_specs=in_specs, out_specs=out_specs, check_vma=False
    )
```
